32 devices in a mesh: server: 4 (over z), worker: 8 (over y, x, core).
Axes of the slice: x: 2, y: 2, z: 4, core: 2. Of those that a mesh axis runs over, the one named last changes fastest.
Arguments:
- sgt: bfloat16 [4096, 18, 2048], P(('server', 'worker')), may hold values from -6 to 6
- ownership: int32 [4096], replicated, may hold values from 0 to 4095, as said below
- sub_points: int32 [8, 4, 96], P('worker', None, 'server'), may hold values from 0 to 4095, as said below
- moments: float32 [8, 4, 6, 96], P('worker', None, None, 'server'), may hold values from -0.25 to 0.25
- slip: bfloat16 [8, 4, 96, 512], P('worker', None, 'server'), may hold values from -0.25 to 0.25
Outputs:
- seismogram: float32 [8, 4, 3, 2048], P('worker', 'server')
- spectra_out: float32 [8, 4, 3, 44], P('worker', 'server')
The draws below stay inside these ranges and needn't reach their ends.
Inputs may be any that keep to these rules, and one draw needn't show every extreme that they name: A permutation: fault point p is stored in row ownership[p] of sgt, which lies on the device of index ownership[p] // 128 along server+worker. `sub_points`: of the 96 subfaults that one device holds (4 ruptures times 24 subfaults), at most 4 are stored on any one device, and that number is reached; a point may recur.
All inputs are finite; a program needn't handle non-finite values.
Results may differ from the reference program's by a relative error of at most 0.0043.
Values may be sent and summed in bfloat16 or wider, within the bound.
No kernel may reach another device: no remote copies, remote signals or barrier semaphores. Data moves between devices by JAX's collectives and lax.ppermute only.
A program may use at most 192 MiB of HBM per device.

```python
import math
import jax
import jax.numpy as jnp
from jax import lax

NT = 2048
NF = 1024
NS = 512
PERIODS = 44
PTS_DEV = 128
KS = 24
RUP_W = 4
NWR = 8
K = 96
REQ = 96
CAP = 4
NPTS = 4096
N_SERVER = 4
N_WORKER = 8


def common_layout(key):
    base = jax.random.fold_in(key, 7)
    keys = jax.random.split(base, 4)
    ownership = jax.random.permutation(keys[0], NPTS).astype(jnp.int32)
    occupant = jnp.zeros((NPTS,), jnp.int32).at[ownership].set(jnp.arange(NPTS, dtype=jnp.int32))
    n_devices = N_SERVER * N_WORKER
    hot_order = jax.random.permutation(keys[1], n_devices).astype(jnp.int32)
    owners = jnp.concatenate([jnp.repeat(hot_order[:n_devices // 2], CAP), jnp.repeat(hot_order[n_devices // 2:], CAP // 2)])
    device_keys = jax.random.split(keys[2], n_devices)

    def shuffle_one(device_key):
        return jax.random.permutation(device_key, owners)
    shuffled = jax.vmap(shuffle_one)(device_keys).astype(jnp.int32)
    local_rows = jax.random.randint(keys[3], (n_devices, REQ), 0, PTS_DEV).astype(jnp.int32)
    slots = shuffled * PTS_DEV + local_rows
    points = occupant[slots]
    layout = jnp.transpose(points.reshape(N_SERVER, N_WORKER, RUP_W, KS), (1, 2, 0, 3)).reshape(NWR, RUP_W, K)
    return (ownership, layout)


def draw_ownership(key, part):
    return common_layout(key)[0]


def draw_sub_points(key, part):
    return common_layout(key)[1]


def block_scale(key, shape, cuts, least, high):
    def one(dim, blocks):
        draws = jax.random.uniform(jax.random.fold_in(jax.random.fold_in(key, 6), dim), (blocks,), jnp.float32, least / len(cuts), high / len(cuts))
        return jnp.repeat(jnp.exp(draws), shape[dim] // blocks).reshape((-1,) + (1,) * (len(shape) - dim - 1))

    gain = one(*cuts[0])
    for cut in cuts[1:]:
        gain = gain * one(*cut)
    return gain


def gaussian(stream_key, dims, spread, bound, cuts=(), kind=jnp.bfloat16):
    loudness = block_scale(stream_key, dims, cuts, -0.22, 0.18) if cuts else 1.0
    entries = jax.random.normal(stream_key, dims, jnp.float32) * spread * loudness
    return jnp.minimum(jnp.maximum(entries, -bound), bound).astype(kind)


def setup_inputs(seed: int = 0) -> dict:
    seeds = jax.random.split(jax.random.key(seed), 6)
    sgt = gaussian(seeds[0], (NPTS, 18, NT), 1.0, 6.0, ((0, 32),))
    ownership = draw_ownership(jax.random.fold_in(seeds[5], 71), 0)
    sub_points = draw_sub_points(jax.random.fold_in(seeds[5], 71), 0)
    moments = gaussian(seeds[3], (NWR, RUP_W, 6, K), (6 * K) ** -0.5, 0.25, ((0, 8), (3, 4)), jnp.float32)
    slip = gaussian(seeds[4], (NWR, RUP_W, K, NS), NS ** -0.5, 0.25, ((0, 8), (2, 4)))
    return {"sgt": sgt, "ownership": ownership, "sub_points": sub_points, "moments": moments, "slip": slip}


DAMPING = 0.05


def dft_tables(n_time):
    n_freq = n_time // 2
    time_index = jnp.arange(n_time, dtype=jnp.int32)
    freq_index = jnp.arange(n_freq, dtype=jnp.int32)
    wrapped = (time_index[:, None] * freq_index[None, :]) % n_time
    angles = wrapped.astype(jnp.float32) * (2.0 * math.pi / n_time)
    forward = jnp.concatenate([jnp.cos(angles), -jnp.sin(angles)], axis=1).astype(jnp.bfloat16)
    weight = jnp.where(freq_index == 0, 1.0, 2.0).astype(jnp.float32)
    inverse = jnp.concatenate([weight[:, None] * jnp.cos(angles.T), -weight[:, None] * jnp.sin(angles.T)], axis=0)
    return forward, inverse


def oscillator_peaks(spec, inverse, n_time, n_periods):
    n_freq = n_time // 2
    omega_freq = jnp.arange(n_freq, dtype=jnp.int32).astype(jnp.float32) * (2.0 * math.pi / n_time)
    low = math.log(4.0 / n_time)
    high = math.log(0.25)
    steps_osc = jnp.arange(n_periods, dtype=jnp.int32).astype(jnp.float32)
    omega_osc = 2.0 * math.pi * jnp.exp(low + (high - low) * steps_osc / (n_periods - 1))
    den_real = omega_osc[:, None] ** 2 - omega_freq[None, :] ** 2
    den_imag = 2.0 * DAMPING * omega_osc[:, None] * omega_freq[None, :]
    den_square = den_real * den_real + den_imag * den_imag
    gain_osc = omega_osc[:, None] ** 2 / den_square
    spec_real = spec[:, None, :n_freq]
    spec_imag = spec[:, None, n_freq:]
    acc_real = -gain_osc * (spec_real * den_real + spec_imag * den_imag)
    acc_imag = -gain_osc * (spec_imag * den_real - spec_real * den_imag)
    stacked = jnp.concatenate([acc_real, acc_imag], axis=-1).reshape(3 * n_periods, n_time)
    accel = jnp.dot(stacked, inverse, precision=lax.Precision.HIGHEST) / n_time
    return jnp.max(jnp.abs(accel), axis=-1).reshape(3, n_periods)


def contract_moment(green_rows, weight_rows):
    count = green_rows.shape[0]
    n_time = green_rows.shape[-1]
    shaped = green_rows.reshape(count, 3, 6, n_time)
    summed = jnp.zeros((count, 3, n_time), jnp.float32)
    for component in range(6):
        summed = summed + weight_rows[:, component][:, None, None] * shaped[:, :, component, :].astype(jnp.float32)
    return summed.astype(jnp.bfloat16)


def reference(sgt, ownership, sub_points, moments, slip):
    forward, inverse = dft_tables(NT)
    ruptures = NWR * RUP_W
    point_ids = sub_points.reshape(ruptures, K)
    moment_rows = jnp.transpose(moments.reshape(ruptures, 6, K), (0, 2, 1))
    slip_rows = slip.reshape(ruptures, K, NS)

    def one_rupture(inputs):
        points_now, weights_now, slip_now = inputs
        green_rows = sgt[ownership[points_now]]
        traces = contract_moment(green_rows, weights_now).reshape(K * 3, NT)
        trace_spec = jnp.dot(traces, forward, preferred_element_type=jnp.float32).reshape(K, 3, NT)
        slip_spec = jnp.dot(slip_now, forward[:NS], preferred_element_type=jnp.float32)[:, None, :]
        real_part = jnp.sum(slip_spec[..., :NF] * trace_spec[..., :NF] - slip_spec[..., NF:] * trace_spec[..., NF:], axis=0)
        imag_part = jnp.sum(slip_spec[..., :NF] * trace_spec[..., NF:] + slip_spec[..., NF:] * trace_spec[..., :NF], axis=0)
        spec = jnp.concatenate([real_part, imag_part], axis=-1)
        seismo = jnp.dot(spec, inverse, precision=lax.Precision.HIGHEST) / NT
        peaks = oscillator_peaks(spec, inverse, NT, PERIODS)
        return seismo, peaks

    seismo, peaks = lax.map(one_rupture, (point_ids, moment_rows, slip_rows))
    return seismo.reshape(NWR, RUP_W, 3, NT), peaks.reshape(NWR, RUP_W, 3, PERIODS)
```

```python
import functools
import math

import jax
import jax.numpy as jnp
import numpy as np
from jax import lax
from jax.experimental import pallas as pl
from jax.experimental.pallas import tpu as pltpu
from jax.sharding import PartitionSpec as P

PERIODS = 44
DAMPING = 0.05
ROWS = 48
GROUP = 8
PAD = 32
STEP = 32
F32 = jnp.float32
BF16 = jnp.bfloat16


def nn(a, b):
    return lax.dot_general(a, b, (((1,), (0,)), ((), ())), preferred_element_type=F32)


def nt(a, b):
    return lax.dot_general(a, b, (((1,), (1,)), ((), ())), preferred_element_type=F32)


def iota(shape, dim):
    return lax.broadcasted_iota(jnp.int32, shape, dim)


def hilo(x):
    hi = x.astype(BF16)
    return hi, (x - hi.astype(F32)).astype(BF16)


def angle(product, n_time):
    return (2.0 * math.pi / n_time) * (product % n_time)


def forward_bases(n_time):
    half = n_time // 2
    quarter = half // 2
    freq = np.concatenate([2 * np.arange(quarter), 2 * np.arange(quarter) + 1])
    coarse = angle(np.arange(half // STEP)[:, None] * STEP * freq[None, :], n_time)
    fine = angle(np.arange(STEP)[:, None] * freq[None, :], n_time)
    return [f(x).astype(np.float32) for x in (coarse, fine) for f in (np.cos, np.sin)]


def inverse_bases(n_time):
    half = n_time // 2
    quarter = half // 2
    time = np.arange(half)
    coarse = angle(np.arange(quarter // STEP)[:, None] * 2 * STEP * time[None, :], n_time)
    even = angle(np.arange(STEP)[:, None] * 2 * time[None, :], n_time)
    odd = angle((np.arange(STEP)[:, None] * 2 + 1) * time[None, :], n_time)
    return [f(x).astype(np.float32) for x in (coarse, even, odd) for f in (np.cos, np.sin)]


def pack_kernel(capacity, own_ref, pts_ref, mom_ref, slip_ref, out_ref, scr):
    devices = out_ref.shape[0]
    slots = devices * capacity
    rup_w, sub = pts_ref.shape
    n_slip = slip_ref.shape[2]
    own = own_ref[...]
    blocks = own.shape[0]
    both = jnp.concatenate([own // 128, own % 128], axis=0).astype(F32).astype(BF16)
    spread = iota((128, 6), 0)
    comp = iota((128, 6), 1)
    spread_hi = ((spread < 18) & (spread % 6 == comp)).astype(F32).astype(BF16)
    spread_lo = ((spread >= PAD) & (spread < PAD + 18) & ((spread - PAD) % 6 == comp)).astype(F32).astype(BF16)
    earlier = (iota((sub, sub), 0) < iota((sub, sub), 1)).astype(F32).astype(BF16)
    carry = jnp.zeros((devices, 1), F32)
    slip_acc = jnp.zeros((slots, n_slip), F32)
    tail_acc = jnp.zeros((slots, 128), F32)
    lane = iota((slots, 128), 1)
    for r in range(rup_w):
        p = pts_ref[r : r + 1, :]
        in_lane = (iota((128, sub), 0) == p % 128).astype(F32).astype(BF16)
        found = nn(both, in_lane)
        in_block = (iota((blocks, sub), 0) == p // 128).astype(F32)
        dev = jnp.sum(found[:blocks] * in_block, axis=0, keepdims=True)
        loc = jnp.sum(found[blocks:] * in_block, axis=0, keepdims=True)
        onehot = (iota((devices, sub), 0).astype(F32) == dev).astype(F32)
        before = nn(onehot.astype(BF16), earlier) + carry
        rank = jnp.sum(before * onehot, axis=0, keepdims=True)
        carry = carry + jnp.sum(onehot, axis=1, keepdims=True)
        target = dev * capacity + rank
        pick = (iota((slots, sub), 0).astype(F32) == target).astype(F32)
        pick16 = pick.astype(BF16)
        hi, lo = hilo(mom_ref[r])
        expanded = nn(spread_hi, hi) + nn(spread_lo, lo)
        slip_acc = slip_acc + nn(pick16, slip_ref[r])
        tail = nt(pick16, expanded.astype(BF16))
        row = jnp.sum(pick * loc, axis=1, keepdims=True)
        rup = jnp.sum(pick, axis=1, keepdims=True) * float(r)
        tail = tail + jnp.where((lane >= 64) & (lane < 96), row, 0.0) + jnp.where(lane >= 96, rup, 0.0)
        tail_acc = tail_acc + tail
    scr[:, :n_slip] = slip_acc
    scr[:, n_slip:] = tail_acc
    for d in range(devices):
        out_ref[d] = scr[d * capacity : (d + 1) * capacity, :].astype(BF16)


def owner_kernel(
    n_worker, n_server, rec_ref, sgt_ref, ca_ref, sa_ref, cb_ref, sb_ref, *refs
):
    out_refs = refs[: n_worker]
    rec_s, wb_s, idx_v, idx_s, rows_s, tab_s, tr_s, row_sems, idx_sem = refs[n_worker :]
    devices, capacity, width = rec_ref.shape
    slots = devices * capacity
    n_time = sgt_ref.shape[2]
    half = n_time // 2
    quarter = half // 2
    n_slip = width - 128
    for d in range(devices):
        rec_s[d * capacity : (d + 1) * capacity, :] = rec_ref[d].astype(F32)
    tail = rec_s[:, n_slip:].astype(BF16)
    selector = iota((8, 128), 1)
    row_of = nt((selector == 64).astype(F32).astype(BF16), tail)
    rup_of = nt((selector == 96).astype(F32).astype(BF16), tail)[:1]
    idx_v[...] = row_of.astype(jnp.int32)
    to_smem = pltpu.make_async_copy(idx_v, idx_s, idx_sem)
    to_smem.start()
    to_smem.wait()

    def fetch(s):
        return pltpu.make_async_copy(sgt_ref.at[idx_s[0, s]], rows_s.at[s], row_sems.at[s])

    def start(s, carry):
        fetch(s).start()
        return carry

    lax.fori_loop(0, slots, start, 0)

    l_in = iota((128, GROUP * PAD), 0)
    l_out = iota((128, GROUP * PAD), 1) % PAD
    wb_s[0] = nn(tail, (l_in == l_out).astype(F32).astype(BF16))
    wb_s[1] = nn(tail, (l_in == l_out + PAD).astype(F32).astype(BF16))

    wide = 256
    for lc in range(half // wide):
        sl = slice(lc * wide, (lc + 1) * wide)
        sl2 = slice(half + lc * wide, half + (lc + 1) * wide)
        cb = cb_ref[:, sl]
        sb = sb_ref[:, sl]

        def table(a, carry):
            ca = ca_ref[pl.ds(a, 1), sl]
            sa = sa_ref[pl.ds(a, 1), sl]
            at = pl.ds(pl.multiple_of(a * STEP, STEP), STEP)
            tab_s[at, sl] = (ca * cb - sa * sb).astype(BF16)
            tab_s[at, sl2] = (-(sa * cb + ca * sb)).astype(BF16)
            return carry

        lax.fori_loop(0, half // STEP, table, 0)

    lane = iota((GROUP, GROUP * PAD), 1)
    mine = lane // PAD == iota((GROUP, GROUP * PAD), 0)
    comp = (lane % PAD) // 6
    masks = [mine & (comp == c) for c in range(3)]
    keep = iota((GROUP, PAD, 512), 1) < 18

    def contract(g, carry):
        at = pl.ds(pl.multiple_of(g * GROUP, GROUP), GROUP)
        for i in range(GROUP):
            fetch(g * GROUP + i).wait()
        pieces = [jnp.where(m, wb_s[p, at, :], 0.0) for p in range(2) for m in masks]
        left = jnp.concatenate(pieces, axis=0).astype(BF16)
        for n in range(n_time // 512):
            sl = slice(n * 512, (n + 1) * 512)
            rows = rows_s[at, :, sl]
            rows = jnp.concatenate([rows, jnp.zeros((GROUP, PAD - 18, 512), BF16)], axis=1)
            out = nn(left, rows.reshape(GROUP * PAD, 512))
            both = out[: 3 * GROUP] + out[3 * GROUP :]
            for c in range(3):
                tr_s[c, at, sl] = both[c * GROUP : (c + 1) * GROUP]
        return carry

    lax.fori_loop(0, slots // GROUP, contract, 0)

    ruptures = n_worker * n_server
    shape = (ruptures, slots)
    out_row = iota(shape, 0)
    to_worker = (iota(shape, 1) // capacity) % n_worker
    me_w = lax.axis_index("worker")
    me_s = lax.axis_index("server")
    rup_int = rup_of.astype(jnp.int32)
    where_to = ((to_worker ^ me_w) * n_server) + (rup_int ^ me_s)
    seg = (out_row == where_to).astype(F32).astype(BF16)
    slip = rec_s[:, :n_slip].astype(BF16)
    for q in range(2):
        re = slice(q * quarter, (q + 1) * quarter)
        im = slice(half + q * quarter, half + (q + 1) * quarter)
        slip_re = nn(slip, tab_s[:n_slip, re])
        slip_im = nn(slip, tab_s[:n_slip, im])
        for c in range(3):
            x = jnp.concatenate([tr_s[c, :, :half], tr_s[c, :, half:]], axis=0).astype(BF16)
            u_re = nn(x, tab_s[:, re])
            u_im = nn(x, tab_s[:, im])
            if q == 0:
                t_re = u_re[:slots] + u_re[slots:]
                t_im = u_im[:slots] + u_im[slots:]
            else:
                t_re = u_re[:slots] - u_re[slots:]
                t_im = u_im[:slots] - u_im[slots:]
            for cols, prod in (
                (re, slip_re * t_re - slip_im * t_im),
                (im, slip_re * t_im + slip_im * t_re),
            ):
                hi, lo = hilo(prod)
                total = nn(seg, hi) + nn(seg, lo)
                for k in range(n_worker):
                    ref = out_refs[k]
                    ref[c, :, cols] = total[k * n_server : (k + 1) * n_server].astype(ref.dtype)


def sum_kernel(n_server, *refs):
    own_ref = refs[0]
    out_refs = refs[-n_server:]
    for c in range(3):
        total = own_ref[c]
        for ref in refs[1:-n_server]:
            total = total + ref[c].astype(F32)
        for j in range(n_server):
            out_refs[j][c : c + 1, :] = total[j : j + 1].astype(out_refs[j].dtype)


def table_kernel(cc_ref, sc_ref, ce_ref, se_ref, co_ref, so_ref, hi_ref, lo_ref, gr_ref, gi_ref):
    half = hi_ref.shape[2]
    quarter = half // 2
    n_time = 2 * half
    wide = 256
    for q, (cf_ref, sf_ref) in enumerate(((ce_ref, se_ref), (co_ref, so_ref))):
        for lc in range(half // wide):
            sl = slice(lc * wide, (lc + 1) * wide)
            cf = cf_ref[:, sl]
            sf = sf_ref[:, sl]

            def table(a, carry):
                ca = cc_ref[pl.ds(a, 1), sl]
                sa = sc_ref[pl.ds(a, 1), sl]
                for base, value in ((0, ca * cf - sa * sf), (quarter, -(sa * cf + ca * sf))):
                    at = pl.ds(pl.multiple_of(base + a * STEP, STEP), STEP)
                    hi, lo = hilo(value)
                    hi_ref[q, at, sl] = hi
                    lo_ref[q, at, sl] = lo
                return carry

            lax.fori_loop(0, quarter // STEP, table, 0)
    shape = gr_ref.shape
    low = math.log(4.0 / n_time)
    high = math.log(0.25)
    period = iota(shape, 0)
    slot = iota(shape, 1)
    freq = jnp.where(slot < quarter, 2 * slot, 2 * (slot - quarter) + 1)
    omega_freq = freq.astype(F32) * (2.0 * math.pi / n_time)
    omega_osc = 2.0 * math.pi * jnp.exp(low + (high - low) * period.astype(F32) / (PERIODS - 1))
    den_real = omega_osc * omega_osc - omega_freq * omega_freq
    den_imag = 2.0 * DAMPING * omega_osc * omega_freq
    weight = jnp.where(freq == 0, 1.0, 2.0) / n_time
    gain = weight * (omega_osc * omega_osc / (den_real * den_real + den_imag * den_imag))
    gr_ref[...] = jnp.where(period < PERIODS, -gain * den_real, weight)
    gi_ref[...] = jnp.where(period < PERIODS, -gain * den_imag, 0.0)


def final_kernel(n_server, *refs):
    spec_refs = refs[:n_server]
    hi_ref, lo_ref, gr_ref, gi_ref, seis_ref, peak_ref = refs[n_server:]
    half = hi_ref.shape[2]
    quarter = half // 2
    spec = spec_refs[0][...]
    for ref in spec_refs[1:]:
        spec = spec + ref[...].astype(F32)
    gr = gr_ref[...]
    gi = gi_ref[...]
    sums = []
    for q in range(2):
        cols = slice(q * quarter, (q + 1) * quarter)
        cols_im = slice(half + q * quarter, half + (q + 1) * quarter)
        lefts = []
        for c in range(3):
            re = spec[c : c + 1, cols]
            im = spec[c : c + 1, cols_im]
            g_re = gr[:, cols]
            g_im = gi[:, cols]
            lefts.append(jnp.concatenate([re * g_re + im * g_im, im * g_re - re * g_im], axis=1))
        hi, lo = hilo(jnp.concatenate(lefts, axis=0))
        first = nn(jnp.concatenate([hi, lo], axis=0), hi_ref[q])
        sums.append(first[: 3 * ROWS] + first[3 * ROWS :] + nn(hi, lo_ref[q]))
    even, odd = sums
    peak = jnp.max(jnp.abs(even) + jnp.abs(odd), axis=1, keepdims=True)
    for c in range(3):
        row = c * ROWS + PERIODS
        seis_ref[c : c + 1, :half] = even[row : row + 1] + odd[row : row + 1]
        seis_ref[c : c + 1, half:] = even[row : row + 1] - odd[row : row + 1]
        column = jnp.broadcast_to(peak[c * ROWS : (c + 1) * ROWS], (ROWS, 128))
        column = jnp.concatenate([column, jnp.zeros((128 - ROWS, 128), F32)], axis=0)
        peak_ref[c : c + 1, :] = column.T[:1, :PERIODS]


def vmem():
    return pl.BlockSpec(memory_space=pltpu.VMEM)


def params(mib):
    return pltpu.CompilerParams(vmem_limit_bytes=mib << 20)


def shards(n_server, n_worker, sgt, ownership, sub_points, moments, slip):
    devices = n_server * n_worker
    n_time = sgt.shape[2]
    half = n_time // 2
    rup_w = sub_points.shape[1]
    sub_dev = sub_points.shape[2]
    n_slip = slip.shape[3]
    capacity = 4 * sub_dev // (3 * n_worker)
    slots = devices * capacity
    width = n_slip + 128
    assert rup_w == n_server and sgt.shape[0] == 128 and slots % 16 == 0

    record = pl.pallas_call(
        functools.partial(pack_kernel, capacity),
        out_shape=jax.ShapeDtypeStruct((devices, capacity, width), BF16),
        in_specs=[vmem()] * 4,
        out_specs=vmem(),
        scratch_shapes=[pltpu.VMEM((slots, width), F32)],
        compiler_params=params(32),
        name="pack",
    )(ownership.reshape(-1, 128), sub_points[0], moments[0], slip[0])
    record = lax.all_to_all(record, ("server", "worker"), split_axis=0, concat_axis=0, tiled=True)

    chunk = (3, n_server, n_time)
    sums = pl.pallas_call(
        functools.partial(owner_kernel, n_worker, n_server),
        out_shape=[jax.ShapeDtypeStruct(chunk, BF16 if k else F32) for k in range(n_worker)],
        in_specs=[vmem(), pl.BlockSpec(memory_space=pl.ANY)] + [vmem()] * 4,
        out_specs=[vmem()] * n_worker,
        scratch_shapes=[
            pltpu.VMEM((slots, width), F32),
            pltpu.VMEM((2, slots, GROUP * PAD), F32),
            pltpu.VMEM((8, slots), jnp.int32),
            pltpu.SMEM((8, slots), jnp.int32),
            pltpu.VMEM((slots, 18, n_time), BF16),
            pltpu.VMEM((half, n_time), BF16),
            pltpu.VMEM((3, slots, n_time), F32),
            pltpu.SemaphoreType.DMA((slots,)),
            pltpu.SemaphoreType.DMA,
        ],
        compiler_params=params(56),
        cost_estimate=pl.CostEstimate(flops=10**10, bytes_accessed=2 * 10**7, transcendentals=0),
        name="owner",
    )(record, sgt, *[jnp.asarray(x) for x in forward_bases(n_time)])

    bases, first = lax.optimization_barrier(
        (tuple(jnp.asarray(x) for x in inverse_bases(n_time)), sums[0])
    )
    tables = pl.pallas_call(
        table_kernel,
        out_shape=[jax.ShapeDtypeStruct((2, half, half), BF16)] * 2
        + [jax.ShapeDtypeStruct((ROWS, half), F32)] * 2,
        in_specs=[vmem()] * 6,
        out_specs=[vmem()] * 4,
        compiler_params=params(24),
        cost_estimate=pl.CostEstimate(flops=10**9, bytes_accessed=10**7, transcendentals=0),
        name="inverse_tables",
    )(*bases)

    arrived = [
        lax.ppermute(sums[k], "worker", [(j, j ^ k) for j in range(n_worker)])
        for k in range(1, n_worker)
    ]
    partial = pl.pallas_call(
        functools.partial(sum_kernel, n_server),
        out_shape=[jax.ShapeDtypeStruct((3, n_time), BF16 if j else F32) for j in range(n_server)],
        in_specs=[vmem()] * n_worker,
        out_specs=[vmem()] * n_server,
        compiler_params=params(16),
        name="worker_sum",
    )(first, *arrived)
    arrived = [
        lax.ppermute(partial[j], "server", [(i, i ^ j) for i in range(n_server)])
        for j in range(1, n_server)
    ]
    seis, peaks = pl.pallas_call(
        functools.partial(final_kernel, n_server),
        out_shape=[
            jax.ShapeDtypeStruct((3, n_time), F32),
            jax.ShapeDtypeStruct((3, PERIODS), F32),
        ],
        in_specs=[vmem()] * (n_server + 4),
        out_specs=[vmem()] * 2,
        compiler_params=params(32),
        name="finish",
    )(partial[0], *arrived, *tables)
    return seis.reshape(1, 1, 3, n_time), peaks.reshape(1, 1, 3, PERIODS)


def solution(mesh):
    placed = (
        P(("server", "worker"), None, None),
        P(),
        P("worker", None, "server"),
        P("worker", None, None, "server"),
        P("worker", None, "server", None),
    )
    return jax.shard_map(
        functools.partial(shards, mesh.shape["server"], mesh.shape["worker"]),
        mesh=mesh,
        in_specs=placed,
        out_specs=(P("worker", "server", None, None), P("worker", "server", None, None)),
        check_vma=False,
    )
```

```python
import functools
import math

import jax
import jax.numpy as jnp
import numpy as np
from jax import lax
from jax.experimental import pallas as pl
from jax.experimental.pallas import tpu as pltpu
from jax.sharding import PartitionSpec as P

PERIODS = 44
DAMPING = 0.05
ROWS = 48
STEP = 32
PTS = 128
ROW_LANE = 64
RUP_LANE = 96
F32 = jnp.float32
BF16 = jnp.bfloat16


def nn(a, b):
    return lax.dot_general(a, b, (((1,), (0,)), ((), ())), preferred_element_type=F32)


def nt(a, b):
    return lax.dot_general(a, b, (((1,), (1,)), ((), ())), preferred_element_type=F32)


def iota(shape, dim):
    return lax.broadcasted_iota(jnp.int32, shape, dim)


def hilo(x):
    hi = x.astype(BF16)
    return hi, (x - hi.astype(F32)).astype(BF16)


def angle(product, n_time):
    return (2.0 * math.pi / n_time) * (product % n_time)


def forward_bases(n_time):
    half = n_time // 2
    quarter = half // 2
    freq = np.concatenate([2 * np.arange(quarter), 2 * np.arange(quarter) + 1])
    coarse = angle(np.arange(half // STEP)[:, None] * STEP * freq[None, :], n_time)
    fine = angle(np.arange(STEP)[:, None] * freq[None, :], n_time)
    return np.concatenate([f(x) for x in (coarse, fine) for f in (np.cos, np.sin)]).astype(np.float32)


def inverse_bases(n_time):
    half = n_time // 2
    quarter = half // 2
    time = np.arange(half)
    coarse = angle(np.arange(quarter // STEP)[:, None] * 2 * STEP * time[None, :], n_time)
    even = angle(np.arange(STEP)[:, None] * 2 * time[None, :], n_time)
    odd = angle((np.arange(STEP)[:, None] * 2 + 1) * time[None, :], n_time)
    return [
        np.concatenate([f(x) for x in (coarse, fine) for f in (np.cos, np.sin)]).astype(np.float32)
        for fine in (even, odd)
    ]


def pack_kernel(capacity, own_ref, pts_ref, mom_ref, slip_ref, out_ref, scr):
    devices = out_ref.shape[0]
    slots = devices * capacity
    rup_w, sub = pts_ref.shape
    n_slip = slip_ref.shape[2]
    own = own_ref[...]
    blocks = own.shape[0]
    both = jnp.concatenate([own // PTS, own % PTS], axis=0).astype(F32).astype(BF16)
    spread = iota((128, 6), 0)
    comp = iota((128, 6), 1)
    spread_hi = (spread == comp).astype(F32).astype(BF16)
    spread_lo = (spread == comp + 6).astype(F32).astype(BF16)
    earlier = (iota((sub, sub), 0) < iota((sub, sub), 1)).astype(F32).astype(BF16)
    carry = jnp.zeros((devices, 1), F32)
    slip_acc = jnp.zeros((slots, n_slip), F32)
    tail_acc = jnp.zeros((slots, 128), F32)
    lane = iota((slots, 128), 1)
    for r in range(rup_w):
        p = pts_ref[r : r + 1, :]
        in_lane = (iota((128, sub), 0) == p % 128).astype(F32).astype(BF16)
        found = nn(both, in_lane)
        in_block = (iota((blocks, sub), 0) == p // 128).astype(F32)
        dev = jnp.sum(found[:blocks] * in_block, axis=0, keepdims=True)
        loc = jnp.sum(found[blocks:] * in_block, axis=0, keepdims=True)
        onehot = (iota((devices, sub), 0).astype(F32) == dev).astype(F32)
        before = nn(onehot.astype(BF16), earlier) + carry
        rank = jnp.sum(before * onehot, axis=0, keepdims=True)
        carry = carry + jnp.sum(onehot, axis=1, keepdims=True)
        target = dev * capacity + rank
        pick = (iota((slots, sub), 0).astype(F32) == target).astype(F32)
        pick16 = pick.astype(BF16)
        mom = jnp.concatenate([mom_ref[m, r : r + 1, :] for m in range(6)], axis=0)
        hi, lo = hilo(mom)
        expanded = nn(spread_hi, hi) + nn(spread_lo, lo)
        slip_acc = slip_acc + nn(pick16, slip_ref[r])
        tail = nt(pick16, expanded.astype(BF16))
        row = jnp.sum(pick * loc, axis=1, keepdims=True)
        rup = jnp.sum(pick, axis=1, keepdims=True) * float(r)
        tail = tail + jnp.where(lane == ROW_LANE, row, 0.0) + jnp.where(lane == RUP_LANE, rup, 0.0)
        tail_acc = tail_acc + tail
    scr[:, :n_slip] = slip_acc
    scr[:, n_slip:] = tail_acc
    for d in range(devices):
        out_ref[d] = scr[d * capacity : (d + 1) * capacity, :].astype(BF16)


def owner_kernel(stages, rec_ref, sgt_ref, tab_ref, *refs):
    first = stages[0][1]
    out_refs = refs[:first]
    rec_s, x_s, sgt_s, tab_s, sems = refs[first:]
    devices, capacity, width = rec_ref.shape
    slots = devices * capacity
    n_time = sgt_ref.shape[2]
    half = n_time // 2
    quarter = half // 2
    n_slip = width - 128
    wide = 512

    def rows_copy(c):
        at = slice(6 * c, 6 * c + 6)
        return pltpu.make_async_copy(sgt_ref.at[at], sgt_s.at[at], sems.at[c])

    def table_copy(i):
        at = slice(i * quarter, (i + 1) * quarter)
        return pltpu.make_async_copy(tab_ref.at[:, at], tab_s.at[:, at], sems.at[3 + i])

    for c in range(3):
        rows_copy(c).start()
    for i in (0, 2, 1, 3):
        table_copy(i).start()
    for d in range(devices):
        rec_s[d * capacity : (d + 1) * capacity, :] = rec_ref[d].astype(F32)
    tail = rec_s[:, n_slip:]
    row = tail[:, ROW_LANE : ROW_LANE + 1]
    here = iota((slots, PTS), 1).astype(F32) == row
    left = jnp.concatenate(
        [
            jnp.concatenate(
                [jnp.where(here, tail[:, 6 * p + m : 6 * p + m + 1], 0.0).astype(BF16) for m in range(6)],
                axis=1,
            )
            for p in range(2)
        ],
        axis=0,
    )
    for c in range(3):
        rows_copy(c).wait()
        for n in range(n_time // wide):
            rows = sgt_s[6 * c : 6 * c + 6, :, n * wide : (n + 1) * wide].reshape(6 * PTS, wide)
            out = nn(left, rows)
            h, at = divmod(n * wide, half)
            x_s[c, h * slots : (h + 1) * slots, at : at + wide] = (out[:slots] + out[slots:]).astype(BF16)

    ruptures = math.prod(radix for _, radix, _, _ in stages)
    shape = (ruptures, slots)
    rup = nt((iota((8, 128), 1) == RUP_LANE).astype(F32).astype(BF16), tail.astype(BF16))[:1].astype(jnp.int32)
    worker = (iota((1, slots), 1) // capacity) % lax.axis_size("worker")
    apart = {"worker": worker ^ lax.axis_index("worker"), "server": rup ^ lax.axis_index("server")}
    where_to = jnp.zeros((1, slots), jnp.int32)
    for axis, radix, shift, _ in stages:
        where_to = where_to * radix + ((apart[axis] >> shift) & (radix - 1))
    seg = (iota(shape, 0) == where_to).astype(F32).astype(BF16)
    slip = rec_s[:, :n_slip].astype(BF16)
    part = ruptures // first
    for q in range(2):
        re = slice(q * quarter, (q + 1) * quarter)
        im = slice(half + q * quarter, half + (q + 1) * quarter)
        table_copy(q).wait()
        table_copy(q + 2).wait()
        slip_re = nn(slip, tab_s[:n_slip, re])
        slip_im = nn(slip, tab_s[:n_slip, im])
        for c in range(3):
            x = x_s[c]
            u_re = nn(x, tab_s[:, re])
            u_im = nn(x, tab_s[:, im])
            if q == 0:
                t_re = u_re[:slots] + u_re[slots:]
                t_im = u_im[:slots] + u_im[slots:]
            else:
                t_re = u_re[:slots] - u_re[slots:]
                t_im = u_im[:slots] - u_im[slots:]
            for cols, prod in (
                (re, slip_re * t_re - slip_im * t_im),
                (im, slip_re * t_im + slip_im * t_re),
            ):
                hi, lo = hilo(prod)
                total = nn(seg, hi) + nn(seg, lo)
                for k in range(first):
                    ref = out_refs[k]
                    ref[c, :, cols] = total[k * part : (k + 1) * part].astype(ref.dtype)


def sum_kernel(radix, *refs):
    own_ref = refs[0]
    out_refs = refs[-radix:]
    part = out_refs[0].shape[1]
    for c in range(3):
        total = own_ref[c]
        for ref in refs[1:-radix]:
            total = total + ref[c].astype(F32)
        for k in range(radix):
            out_refs[k][c] = total[k * part : (k + 1) * part].astype(out_refs[k].dtype)


def forward_table_kernel(base_ref, tab_ref):
    half = tab_ref.shape[0]
    count = half // STEP
    wide = 256
    for lc in range(half // wide):
        sl = slice(lc * wide, (lc + 1) * wide)
        sl2 = slice(half + lc * wide, half + (lc + 1) * wide)
        cb = base_ref[2 * count : 2 * count + STEP, sl]
        sb = base_ref[2 * count + STEP :, sl]

        def table(a, carry):
            ca = base_ref[pl.ds(a, 1), sl]
            sa = base_ref[pl.ds(count + a, 1), sl]
            at = pl.ds(pl.multiple_of(a * STEP, STEP), STEP)
            tab_ref[at, sl] = (ca * cb - sa * sb).astype(BF16)
            tab_ref[at, sl2] = (-(sa * cb + ca * sb)).astype(BF16)
            return carry

        lax.fori_loop(0, half // STEP, table, 0)


def inverse_table_kernel(base_ref, hi_ref, lo_ref):
    half = hi_ref.shape[0]
    quarter = half // 2
    count = quarter // STEP
    wide = 256
    for lc in range(half // wide):
        sl = slice(lc * wide, (lc + 1) * wide)
        cf = base_ref[2 * count : 2 * count + STEP, sl]
        sf = base_ref[2 * count + STEP :, sl]

        def table(a, carry):
            ca = base_ref[pl.ds(a, 1), sl]
            sa = base_ref[pl.ds(count + a, 1), sl]
            for base, value in ((0, ca * cf - sa * sf), (quarter, -(sa * cf + ca * sf))):
                at = pl.ds(pl.multiple_of(base + a * STEP, STEP), STEP)
                hi, lo = hilo(value)
                hi_ref[at, sl] = hi
                lo_ref[at, sl] = lo
            return carry

        lax.fori_loop(0, count, table, 0)


def gain_kernel(gr_ref, gi_ref):
    half = gr_ref.shape[1]
    quarter = half // 2
    n_time = 2 * half
    shape = gr_ref.shape
    low = math.log(4.0 / n_time)
    high = math.log(0.25)
    period = iota(shape, 0)
    slot = iota(shape, 1)
    freq = jnp.where(slot < quarter, 2 * slot, 2 * (slot - quarter) + 1)
    omega_freq = freq.astype(F32) * (2.0 * math.pi / n_time)
    omega_osc = 2.0 * math.pi * jnp.exp(low + (high - low) * period.astype(F32) / (PERIODS - 1))
    den_real = omega_osc * omega_osc - omega_freq * omega_freq
    den_imag = 2.0 * DAMPING * omega_osc * omega_freq
    weight = jnp.where(freq == 0, 1.0, 2.0) / n_time
    gain = weight * (omega_osc * omega_osc / (den_real * den_real + den_imag * den_imag))
    gr_ref[...] = jnp.where(period < PERIODS, -gain * den_real, weight)
    gi_ref[...] = jnp.where(period < PERIODS, -gain * den_imag, 0.0)


def final_kernel(count, *refs):
    spec_refs = refs[:count]
    *tables, gr_ref, gi_ref, seis_ref, peak_ref = refs[count:]
    half = gr_ref.shape[1]
    quarter = half // 2
    spec = []
    for c in range(3):
        total = spec_refs[0][c]
        for ref in spec_refs[1:]:
            total = total + ref[c].astype(F32)
        spec.append(total)
    gr = gr_ref[...]
    gi = gi_ref[...]
    sums = []
    for q in range(2):
        cols = slice(q * quarter, (q + 1) * quarter)
        cols_im = slice(half + q * quarter, half + (q + 1) * quarter)
        lefts = []
        for c in range(3):
            re = spec[c][:, cols]
            im = spec[c][:, cols_im]
            g_re = gr[:, cols]
            g_im = gi[:, cols]
            lefts.append(jnp.concatenate([re * g_re + im * g_im, im * g_re - re * g_im], axis=1))
        hi, lo = hilo(jnp.concatenate(lefts, axis=0))
        hi_ref, lo_ref = tables[2 * q : 2 * q + 2]
        first = nn(jnp.concatenate([hi, lo], axis=0), hi_ref[...])
        sums.append(first[: 3 * ROWS] + first[3 * ROWS :] + nn(hi, lo_ref[...]))
    even, odd = sums
    peak = jnp.max(jnp.abs(even) + jnp.abs(odd), axis=1, keepdims=True)
    for c in range(3):
        row = c * ROWS + PERIODS
        seis_ref[c, :, :half] = even[row : row + 1] + odd[row : row + 1]
        seis_ref[c, :, half:] = even[row : row + 1] - odd[row : row + 1]
        column = jnp.broadcast_to(peak[c * ROWS : (c + 1) * ROWS], (ROWS, 128))
        column = jnp.concatenate([column, jnp.zeros((128 - ROWS, 128), F32)], axis=0)
        peak_ref[c] = column.T[:1, :PERIODS]


def vmem():
    return pl.BlockSpec(memory_space=pltpu.VMEM)


def params(mib):
    return pltpu.CompilerParams(vmem_limit_bytes=mib << 20)


def exchange_plan(n_worker, n_server):
    stages = []
    for axis, size in (("worker", n_worker), ("server", n_server)):
        bits = size.bit_length() - 1
        assert size == 1 << bits
        shift = 0
        while shift < bits:
            step = 1 if (bits - shift) % 2 else 2
            stages.append((axis, 1 << step, shift, size))
            shift += step
    return stages


def send(parts, stage):
    axis, radix, shift, size = stage
    return [
        lax.ppermute(parts[k], axis, [(i, i ^ (k << shift)) for i in range(size)])
        for k in range(1, radix)
    ]


def sent_type(stages, i):
    return F32 if i == 0 or i == len(stages) - 1 else BF16


def shards(n_server, n_worker, sgt, ownership, sub_points, moments, slip):
    devices = n_server * n_worker
    n_time = sgt.shape[2]
    half = n_time // 2
    rup_w = sub_points.shape[1]
    sub_dev = sub_points.shape[2]
    n_slip = slip.shape[3]
    capacity = 4 * sub_dev // (3 * n_worker)
    slots = devices * capacity
    width = n_slip + 128
    stages = exchange_plan(n_worker, n_server)
    assert rup_w == n_server and sgt.shape[0] == PTS and slots % 16 == 0

    record = pl.pallas_call(
        functools.partial(pack_kernel, capacity),
        out_shape=jax.ShapeDtypeStruct((devices, capacity, width), BF16),
        in_specs=[vmem()] * 4,
        out_specs=vmem(),
        scratch_shapes=[pltpu.VMEM((slots, width), F32)],
        compiler_params=params(56),
        name="pack",
    )(ownership.reshape(-1, 128), sub_points[0], jnp.transpose(moments[0], (1, 0, 2)), slip[0])
    record = lax.all_to_all(record, ("server", "worker"), split_axis=0, concat_axis=0, tiled=True)

    table = pl.pallas_call(
        forward_table_kernel,
        out_shape=jax.ShapeDtypeStruct((half, n_time), BF16),
        in_specs=[vmem()],
        out_specs=vmem(),
        compiler_params=params(8),
        cost_estimate=pl.CostEstimate(flops=10**9, bytes_accessed=10**7, transcendentals=0),
        name="forward_table",
    )(jnp.asarray(forward_bases(n_time)))
    bases = [jnp.asarray(x) for x in inverse_bases(n_time)]
    inverse = pl.pallas_call(
        inverse_table_kernel,
        out_shape=[jax.ShapeDtypeStruct((half, half), BF16)] * 2,
        in_specs=[vmem()],
        out_specs=[vmem()] * 2,
        compiler_params=params(8),
        cost_estimate=pl.CostEstimate(flops=10**9, bytes_accessed=10**7, transcendentals=0),
        name="inverse_table",
    )
    gain = pl.pallas_call(
        gain_kernel,
        out_shape=[jax.ShapeDtypeStruct((ROWS, half), F32)] * 2,
        out_specs=[vmem()] * 2,
        compiler_params=params(2),
        name="gain",
    )()
    tables = []

    def part_shapes(i):
        count = math.prod(radix for _, radix, _, _ in stages[i + 1 :])
        return [
            jax.ShapeDtypeStruct((3, count, n_time), sent_type(stages, i) if k else F32)
            for k in range(stages[i][1])
        ]

    parts = pl.pallas_call(
        functools.partial(owner_kernel, stages),
        out_shape=part_shapes(0),
        in_specs=[vmem(), pl.BlockSpec(memory_space=pl.ANY), pl.BlockSpec(memory_space=pl.ANY)],
        out_specs=[vmem()] * stages[0][1],
        scratch_shapes=[
            pltpu.VMEM((slots, width), F32),
            pltpu.VMEM((3, 2 * slots, half), BF16),
            pltpu.VMEM((18, PTS, n_time), BF16),
            pltpu.VMEM((half, n_time), BF16),
            pltpu.SemaphoreType.DMA((7,)),
        ],
        compiler_params=params(52),
        cost_estimate=pl.CostEstimate(flops=10**10, bytes_accessed=2 * 10**7, transcendentals=0),
        name="owner",
    )(record, jnp.transpose(sgt, (1, 0, 2)), table)
    arrived = send(parts, stages[0])
    for i in range(1, len(stages)):
        radix = stages[i][1]
        parts = pl.pallas_call(
            functools.partial(sum_kernel, radix),
            out_shape=part_shapes(i),
            in_specs=[vmem()] * (1 + len(arrived)),
            out_specs=[vmem()] * radix,
            compiler_params=params(4),
            name=f"sum_{i}",
        )(parts[0], *arrived)
        arrived = send(parts, stages[i])
        if i >= len(stages) - 2:
            base, own = lax.optimization_barrier((bases[len(tables) // 2], parts[0]))
            pair = inverse(base)
            tables += pair
            own, *pair = lax.optimization_barrier((own, *pair))
            parts = [own]
            tables = tables[:-2] + pair
    count = 1 + len(arrived)
    seis, peaks = pl.pallas_call(
        functools.partial(final_kernel, count),
        out_shape=[
            jax.ShapeDtypeStruct((3, 1, n_time), F32),
            jax.ShapeDtypeStruct((3, 1, PERIODS), F32),
        ],
        in_specs=[vmem()] * (count + 6),
        out_specs=[vmem()] * 2,
        compiler_params=params(20),
        name="finish",
    )(parts[0], *arrived, *tables, *gain)
    return (
        jnp.transpose(seis, (1, 0, 2)).reshape(1, 1, 3, n_time),
        jnp.transpose(peaks, (1, 0, 2)).reshape(1, 1, 3, PERIODS),
    )


def solution(mesh):
    placed = (
        P(("server", "worker"), None, None),
        P(),
        P("worker", None, "server"),
        P("worker", None, None, "server"),
        P("worker", None, "server", None),
    )
    return jax.shard_map(
        functools.partial(shards, mesh.shape["server"], mesh.shape["worker"]),
        mesh=mesh,
        in_specs=placed,
        out_specs=(P("worker", "server", None, None), P("worker", "server", None, None)),
        check_vma=False,
    )
```

```python
import functools
import math

import jax
import jax.numpy as jnp
import numpy as np
from jax import lax
from jax.experimental import pallas as pl
from jax.experimental.pallas import tpu as pltpu
from jax.sharding import PartitionSpec as P

PERIODS = 44
DAMPING = 0.05
ROWS = 48
STEP = 32
PTS = 128
ROW_LANE = 64
RUP_LANE = 96
F32 = jnp.float32
BF16 = jnp.bfloat16


def nn(a, b):
    return lax.dot_general(a, b, (((1,), (0,)), ((), ())), preferred_element_type=F32)


def nt(a, b):
    return lax.dot_general(a, b, (((1,), (1,)), ((), ())), preferred_element_type=F32)


def iota(shape, dim):
    return lax.broadcasted_iota(jnp.int32, shape, dim)


def hilo(x):
    hi = x.astype(BF16)
    return hi, (x - hi.astype(F32)).astype(BF16)


def angle(product, n_time):
    return (2.0 * math.pi / n_time) * (product % n_time)


def forward_bases(n_time):
    half = n_time // 2
    quarter = half // 2
    bases = []
    for odd in range(2):
        freq = 2 * np.arange(quarter) + odd
        coarse = angle(np.arange(half // STEP)[:, None] * STEP * freq[None, :], n_time)
        fine = angle(np.arange(STEP)[:, None] * freq[None, :], n_time)
        bases.append(
            np.concatenate([f(x) for x in (coarse, fine) for f in (np.cos, np.sin)]).astype(np.float32)
        )
    return bases


def inverse_bases(n_time):
    half = n_time // 2
    quarter = half // 2
    time = np.arange(half)
    coarse = angle(np.arange(quarter // STEP)[:, None] * 2 * STEP * time[None, :], n_time)
    even = angle(np.arange(STEP)[:, None] * 2 * time[None, :], n_time)
    odd = angle((np.arange(STEP)[:, None] * 2 + 1) * time[None, :], n_time)
    return [
        np.concatenate([f(x) for x in (coarse, fine) for f in (np.cos, np.sin)]).astype(np.float32)
        for fine in (even, odd)
    ]


def ordered(stages, apart):
    place = jnp.zeros_like(apart["worker"])
    for axis, radix, shift, _ in stages:
        place = place * radix + ((apart[axis] >> shift) & (radix - 1))
    return place


def pack_kernel(stages, capacity, *refs):
    sources, refs = refs[:4], refs[4:]
    first = stages[0][1]
    out_refs = refs[:first]
    scr, own_ref, pts_ref, mom_ref, slip_ref, sems = refs[first:]
    copies = [
        pltpu.make_async_copy(src, dst, sems.at[i])
        for i, (src, dst) in enumerate(zip(sources, (own_ref, pts_ref, mom_ref, slip_ref)))
    ]
    for copy in copies:
        copy.start()
    devices = math.prod(radix for _, radix, _, _ in stages)
    n_worker = lax.axis_size("worker")
    me = lax.axis_index("server") * n_worker + lax.axis_index("worker")
    slots = devices * capacity
    rup_w, sub = pts_ref.shape
    asked = rup_w * sub
    n_slip = slip_ref.shape[2]
    earlier = (iota((asked, asked), 0) < iota((asked, asked), 1)).astype(F32).astype(BF16)
    spread = iota((128, 6), 0)
    comp = iota((128, 6), 1)
    spread_hi = (spread == comp).astype(F32).astype(BF16)
    spread_lo = (spread == comp + 6).astype(F32).astype(BF16)
    for copy in copies:
        copy.wait()
    own = own_ref[...]
    blocks = own.shape[0]
    both = jnp.concatenate([own // PTS, own % PTS], axis=0).astype(F32).astype(BF16)
    p = jnp.concatenate([pts_ref[r : r + 1, :] for r in range(rup_w)], axis=1)
    in_lane = (iota((128, asked), 0) == p % 128).astype(F32).astype(BF16)
    found = nn(both, in_lane)
    in_block = (iota((blocks, asked), 0) == p // 128).astype(F32)
    dev = jnp.sum(found[:blocks] * in_block, axis=0, keepdims=True)
    loc = jnp.sum(found[blocks:] * in_block, axis=0, keepdims=True)
    onehot = (iota((devices, asked), 0).astype(F32) == dev).astype(F32)
    before = nn(onehot.astype(BF16), earlier)
    rank = jnp.sum(before * onehot, axis=0, keepdims=True)
    away = dev.astype(jnp.int32) ^ me
    chunk = ordered(stages, {"worker": away % n_worker, "server": away // n_worker})
    target = chunk.astype(F32) * capacity + rank
    pick = (iota((slots, asked), 0).astype(F32) == target).astype(F32)
    pick16 = pick.astype(BF16)
    mom = jnp.concatenate(
        [
            jnp.concatenate([mom_ref[m, r : r + 1, :] for r in range(rup_w)], axis=1)
            for m in range(6)
        ],
        axis=0,
    )
    hi, lo = hilo(mom)
    rup = (iota((1, asked), 1) // sub).astype(F32)
    lane = iota((128, asked), 0)
    expanded = nn(spread_hi, hi) + nn(spread_lo, lo)
    expanded = jnp.where(lane == ROW_LANE, loc, jnp.where(lane == RUP_LANE, rup, expanded))
    scr[:, n_slip:] = nt(pick16, expanded.astype(BF16))
    slip = slip_ref[...].astype(F32).reshape(asked, n_slip).astype(BF16)
    scr[:, :n_slip] = nn(pick16, slip)
    part = out_refs[0].shape[0]
    for d in range(devices):
        out_refs[d // part][d % part] = scr[d * capacity : (d + 1) * capacity, :].astype(BF16)


def pass_kernel(seen, count, *refs):
    radix = len(refs) - count
    in_refs, out_refs = refs[:count], refs[count:]
    rest = in_refs[0].shape[0] // (seen * radix)
    for o in range(seen):
        for k in range(radix):
            for j in range(rest):
                for i in range(count):
                    at = (o * count + i) * rest + j
                    out_refs[k][at] = in_refs[i][(o * radix + k) * rest + j]


def owner_kernel(stages, sgt_ref, even_ref, odd_ref, *refs):
    first = stages[0][1]
    last = stages[-1][1]
    rec_refs = refs[:last]
    out_refs = refs[last : last + first]
    rec_s, x_s, sgt_s, sems = refs[last + first :]
    part, capacity, width = rec_refs[0].shape
    devices = last * part
    slots = devices * capacity
    n_time = sgt_ref.shape[2]
    half = n_time // 2
    quarter = half // 2
    n_slip = width - 128
    wide = 512
    steps = n_time // wide

    def rows_copy(c, n):
        at = (slice(6 * c, 6 * c + 6), slice(None), slice(n * wide, (n + 1) * wide))
        return pltpu.make_async_copy(sgt_ref.at[at], sgt_s.at[at], sems.at[c * steps + n])

    for c in range(3):
        for n in range(steps):
            rows_copy(c, n).start()
    for d in range(devices):
        rec_s[d * capacity : (d + 1) * capacity, :] = rec_refs[d // part][d % part].astype(F32)
    tail = rec_s[:, n_slip:]
    row = tail[:, ROW_LANE : ROW_LANE + 1]
    here = iota((slots, PTS), 1).astype(F32) == row
    left = jnp.concatenate(
        [
            jnp.concatenate(
                [jnp.where(here, tail[:, 6 * p + m : 6 * p + m + 1], 0.0).astype(BF16) for m in range(6)],
                axis=1,
            )
            for p in range(2)
        ],
        axis=0,
    )
    for c in range(3):
        for n in range(steps):
            rows_copy(c, n).wait()
            rows = sgt_s[6 * c : 6 * c + 6, :, n * wide : (n + 1) * wide].reshape(6 * PTS, wide)
            out = nn(left, rows)
            h, at = divmod(n * wide, half)
            x_s[c, h * slots : (h + 1) * slots, at : at + wide] = (out[:slots] + out[slots:]).astype(BF16)

    ruptures = math.prod(radix for _, radix, _, _ in stages)
    shape = (ruptures, slots)
    rup = nt((iota((8, 128), 1) == RUP_LANE).astype(F32).astype(BF16), tail.astype(BF16))[:1].astype(jnp.int32)
    chunk = iota((1, slots), 1) // capacity
    apart = {"worker": jnp.zeros_like(chunk), "server": rup ^ lax.axis_index("server")}
    for axis, radix, shift, _ in stages[-2::-1]:
        if axis == "worker":
            apart[axis] = apart[axis] | ((chunk % radix) << shift)
        chunk = chunk // radix
    where_to = ordered(stages, apart)
    seg = (iota(shape, 0) == where_to).astype(F32).astype(BF16)
    slip = rec_s[:, :n_slip].astype(BF16)
    part = ruptures // first
    for q in range(2):
        re = slice(q * quarter, (q + 1) * quarter)
        im = slice(half + q * quarter, half + (q + 1) * quarter)
        tab_ref = (even_ref, odd_ref)[q]
        slip_re = nn(slip, tab_ref[:n_slip, :quarter])
        slip_im = nn(slip, tab_ref[:n_slip, quarter:])
        for c in range(3):
            x = x_s[c]
            u_re = nn(x, tab_ref[:, :quarter])
            u_im = nn(x, tab_ref[:, quarter:])
            if q == 0:
                t_re = u_re[:slots] + u_re[slots:]
                t_im = u_im[:slots] + u_im[slots:]
            else:
                t_re = u_re[:slots] - u_re[slots:]
                t_im = u_im[:slots] - u_im[slots:]
            for cols, prod in (
                (re, slip_re * t_re - slip_im * t_im),
                (im, slip_re * t_im + slip_im * t_re),
            ):
                hi, lo = hilo(prod)
                total = nn(seg, hi) + nn(seg, lo)
                for k in range(first):
                    ref = out_refs[k]
                    ref[c, :, cols] = total[k * part : (k + 1) * part].astype(ref.dtype)


def sum_kernel(radix, *refs):
    own_ref = refs[0]
    out_refs = refs[-radix:]
    part = out_refs[0].shape[1]
    for c in range(3):
        total = own_ref[c]
        for ref in refs[1:-radix]:
            total = total + ref[c].astype(F32)
        for k in range(radix):
            out_refs[k][c] = total[k * part : (k + 1) * part].astype(out_refs[k].dtype)


def forward_table_kernel(base_ref, tab_ref):
    half = tab_ref.shape[0]
    quarter = half // 2
    count = half // STEP
    wide = 256
    for lc in range(quarter // wide):
        sl = slice(lc * wide, (lc + 1) * wide)
        sl2 = slice(quarter + lc * wide, quarter + (lc + 1) * wide)
        cb = base_ref[2 * count : 2 * count + STEP, sl]
        sb = base_ref[2 * count + STEP :, sl]

        def table(a, carry):
            ca = base_ref[pl.ds(a, 1), sl]
            sa = base_ref[pl.ds(count + a, 1), sl]
            at = pl.ds(pl.multiple_of(a * STEP, STEP), STEP)
            tab_ref[at, sl] = (ca * cb - sa * sb).astype(BF16)
            tab_ref[at, sl2] = (-(sa * cb + ca * sb)).astype(BF16)
            return carry

        lax.fori_loop(0, count, table, 0)


def inverse_table_kernel(base_ref, hi_ref, lo_ref):
    half = hi_ref.shape[0]
    quarter = half // 2
    count = quarter // STEP
    wide = 256
    for lc in range(half // wide):
        sl = slice(lc * wide, (lc + 1) * wide)
        cf = base_ref[2 * count : 2 * count + STEP, sl]
        sf = base_ref[2 * count + STEP :, sl]

        def table(a, carry):
            ca = base_ref[pl.ds(a, 1), sl]
            sa = base_ref[pl.ds(count + a, 1), sl]
            for base, value in ((0, ca * cf - sa * sf), (quarter, -(sa * cf + ca * sf))):
                at = pl.ds(pl.multiple_of(base + a * STEP, STEP), STEP)
                hi, lo = hilo(value)
                hi_ref[at, sl] = hi
                lo_ref[at, sl] = lo
            return carry

        lax.fori_loop(0, count, table, 0)


def gain_kernel(gr_ref, gi_ref):
    half = gr_ref.shape[1]
    quarter = half // 2
    n_time = 2 * half
    shape = gr_ref.shape
    low = math.log(4.0 / n_time)
    high = math.log(0.25)
    period = iota(shape, 0)
    slot = iota(shape, 1)
    freq = jnp.where(slot < quarter, 2 * slot, 2 * (slot - quarter) + 1)
    omega_freq = freq.astype(F32) * (2.0 * math.pi / n_time)
    omega_osc = 2.0 * math.pi * jnp.exp(low + (high - low) * period.astype(F32) / (PERIODS - 1))
    den_real = omega_osc * omega_osc - omega_freq * omega_freq
    den_imag = 2.0 * DAMPING * omega_osc * omega_freq
    weight = jnp.where(freq == 0, 1.0, 2.0) / n_time
    gain = weight * (omega_osc * omega_osc / (den_real * den_real + den_imag * den_imag))
    gr_ref[...] = jnp.where(period < PERIODS, -gain * den_real, weight)
    gi_ref[...] = jnp.where(period < PERIODS, -gain * den_imag, 0.0)


def final_kernel(count, *refs):
    spec_refs = refs[:count]
    *tables, gr_ref, gi_ref, seis_ref, peak_ref = refs[count:]
    half = gr_ref.shape[1]
    quarter = half // 2
    spec = []
    for c in range(3):
        total = spec_refs[0][c]
        for ref in spec_refs[1:]:
            total = total + ref[c].astype(F32)
        spec.append(total)
    gr = gr_ref[...]
    gi = gi_ref[...]
    sums = []
    for q in range(2):
        cols = slice(q * quarter, (q + 1) * quarter)
        cols_im = slice(half + q * quarter, half + (q + 1) * quarter)
        lefts = []
        for c in range(3):
            re = spec[c][:, cols]
            im = spec[c][:, cols_im]
            g_re = gr[:, cols]
            g_im = gi[:, cols]
            lefts.append(jnp.concatenate([re * g_re + im * g_im, im * g_re - re * g_im], axis=1))
        hi, lo = hilo(jnp.concatenate(lefts, axis=0))
        hi_ref, lo_ref = tables[2 * q : 2 * q + 2]
        first = nn(jnp.concatenate([hi, lo], axis=0), hi_ref[...])
        sums.append(first[: 3 * ROWS] + first[3 * ROWS :] + nn(hi, lo_ref[...]))
    even, odd = sums
    peak = jnp.max(jnp.abs(even) + jnp.abs(odd), axis=1, keepdims=True)
    for c in range(3):
        row = c * ROWS + PERIODS
        seis_ref[c, :, :half] = even[row : row + 1] + odd[row : row + 1]
        seis_ref[c, :, half:] = even[row : row + 1] - odd[row : row + 1]
        column = jnp.broadcast_to(peak[c * ROWS : (c + 1) * ROWS], (ROWS, 128))
        column = jnp.concatenate([column, jnp.zeros((128 - ROWS, 128), F32)], axis=0)
        peak_ref[c] = column.T[:1, :PERIODS]


def vmem():
    return pl.BlockSpec(memory_space=pltpu.VMEM)


def hbm():
    return pl.BlockSpec(memory_space=pltpu.HBM)


def params(mib):
    return pltpu.CompilerParams(vmem_limit_bytes=mib << 20)


def exchange_plan(n_worker, n_server):
    stages = []
    for axis, size in (("worker", n_worker), ("server", n_server)):
        bits = size.bit_length() - 1
        assert size == 1 << bits
        shift = 0
        while shift < bits:
            step = 1 if (bits - shift) % 2 else 2
            stages.append((axis, 1 << step, shift, size))
            shift += step
    return stages


def send(parts, stage):
    axis, radix, shift, size = stage
    return [
        lax.ppermute(parts[k], axis, [(i, i ^ (k << shift)) for i in range(size)])
        for k in range(1, radix)
    ]


def beside(kernel, base, own):
    base, own = lax.optimization_barrier((jnp.asarray(base), own))
    own, *made = lax.optimization_barrier((own, *kernel(base)))
    return own, made


def sent_type(stages, i):
    return F32 if i == 0 or i == len(stages) - 1 else BF16


def shards(n_server, n_worker, sgt, ownership, sub_points, moments, slip):
    devices = n_server * n_worker
    n_time = sgt.shape[2]
    half = n_time // 2
    rup_w = sub_points.shape[1]
    sub_dev = sub_points.shape[2]
    n_slip = slip.shape[3]
    capacity = 4 * sub_dev // (3 * n_worker)
    slots = devices * capacity
    width = n_slip + 128
    stages = exchange_plan(n_worker, n_server)
    assert rup_w == n_server and sgt.shape[0] == PTS and slots % 16 == 0

    forward = pl.pallas_call(
        forward_table_kernel,
        out_shape=[jax.ShapeDtypeStruct((half, half), BF16)],
        in_specs=[vmem()],
        out_specs=[vmem()],
        compiler_params=params(4),
        cost_estimate=pl.CostEstimate(flops=10**9, bytes_accessed=10**7, transcendentals=0),
        name="forward_table",
    )

    def record_shapes(i):
        chunk = (devices // stages[i][1], capacity, width)
        return [jax.ShapeDtypeStruct(chunk, BF16)] * stages[i][1]

    records = pl.pallas_call(
        functools.partial(pack_kernel, stages, capacity),
        out_shape=record_shapes(0),
        in_specs=[hbm()] * 4,
        out_specs=[vmem()] * stages[0][1],
        scratch_shapes=[
            pltpu.VMEM((slots, width), F32),
            pltpu.VMEM((ownership.shape[0] // 128, 128), jnp.int32),
            pltpu.VMEM((rup_w, sub_dev), jnp.int32),
            pltpu.VMEM((6, rup_w, sub_dev), F32),
            pltpu.VMEM((rup_w, sub_dev, n_slip), BF16),
            pltpu.SemaphoreType.DMA((4,)),
        ],
        compiler_params=params(12),
        name="pack",
    )(
        *[
            pltpu.with_memory_space_constraint(x, pltpu.HBM)
            for x in (
                ownership.reshape(-1, 128),
                sub_points[0],
                jnp.transpose(moments[0], (1, 0, 2)),
                slip[0],
            )
        ]
    )
    seen = 1
    bases = forward_bases(n_time)
    forwards = []
    for i in range(len(stages)):
        arrived = send(records, stages[i])
        own = records[0]
        if i >= len(stages) - 2:
            own, table = beside(forward, bases[len(forwards)], own)
            forwards += table
        records = [own, *arrived]
        if i + 1 < len(stages):
            count = len(records)
            records = pl.pallas_call(
                functools.partial(pass_kernel, seen, count),
                out_shape=record_shapes(i + 1),
                in_specs=[vmem()] * count,
                out_specs=[vmem()] * stages[i + 1][1],
                compiler_params=params(2),
                name=f"pass_{i}",
            )(*records)
            seen *= count

    inverse = pl.pallas_call(
        inverse_table_kernel,
        out_shape=[jax.ShapeDtypeStruct((half, half), BF16)] * 2,
        in_specs=[vmem()],
        out_specs=[vmem()] * 2,
        compiler_params=params(8),
        cost_estimate=pl.CostEstimate(flops=10**9, bytes_accessed=10**7, transcendentals=0),
        name="inverse_table",
    )
    gain = pl.pallas_call(
        gain_kernel,
        out_shape=[jax.ShapeDtypeStruct((ROWS, half), F32)] * 2,
        out_specs=[vmem()] * 2,
        compiler_params=params(2),
        name="gain",
    )()
    tables = []
    bases = inverse_bases(n_time)

    def part_shapes(i):
        count = math.prod(radix for _, radix, _, _ in stages[i + 1 :])
        return [
            jax.ShapeDtypeStruct((3, count, n_time), sent_type(stages, i) if k else F32)
            for k in range(stages[i][1])
        ]

    parts = pl.pallas_call(
        functools.partial(owner_kernel, stages),
        out_shape=part_shapes(0),
        in_specs=[hbm()] + [vmem()] * (2 + stages[-1][1]),
        out_specs=[vmem()] * stages[0][1],
        scratch_shapes=[
            pltpu.VMEM((slots, width), F32),
            pltpu.VMEM((3, 2 * slots, half), BF16),
            pltpu.VMEM((18, PTS, n_time), BF16),
            pltpu.SemaphoreType.DMA((12,)),
        ],
        compiler_params=params(32),
        cost_estimate=pl.CostEstimate(flops=10**10, bytes_accessed=2 * 10**7, transcendentals=0),
        name="owner",
    )(pltpu.with_memory_space_constraint(jnp.transpose(sgt, (1, 0, 2)), pltpu.HBM), *forwards, *records)
    arrived = send(parts, stages[0])
    for i in range(1, len(stages)):
        radix = stages[i][1]
        parts = pl.pallas_call(
            functools.partial(sum_kernel, radix),
            out_shape=part_shapes(i),
            in_specs=[vmem()] * (1 + len(arrived)),
            out_specs=[vmem()] * radix,
            compiler_params=params(4),
            name=f"sum_{i}",
        )(parts[0], *arrived)
        arrived = send(parts, stages[i])
        if i >= len(stages) - 2:
            own, pair = beside(inverse, bases[len(tables) // 2], parts[0])
            parts = [own]
            tables += pair
    count = 1 + len(arrived)
    seis, peaks = pl.pallas_call(
        functools.partial(final_kernel, count),
        out_shape=[
            jax.ShapeDtypeStruct((3, 1, n_time), F32),
            jax.ShapeDtypeStruct((3, 1, PERIODS), F32),
        ],
        in_specs=[vmem()] * (count + 6),
        out_specs=[vmem()] * 2,
        compiler_params=params(20),
        name="finish",
    )(parts[0], *arrived, *tables, *gain)
    return (
        jnp.transpose(seis, (1, 0, 2)).reshape(1, 1, 3, n_time),
        jnp.transpose(peaks, (1, 0, 2)).reshape(1, 1, 3, PERIODS),
    )


def solution(mesh):
    placed = (
        P(("server", "worker"), None, None),
        P(),
        P("worker", None, "server"),
        P("worker", None, None, "server"),
        P("worker", None, "server", None),
    )
    return jax.shard_map(
        functools.partial(shards, mesh.shape["server"], mesh.shape["worker"]),
        mesh=mesh,
        in_specs=placed,
        out_specs=(P("worker", "server", None, None), P("worker", "server", None, None)),
        check_vma=False,
    )
```

```python
import functools
import math

import jax
import jax.numpy as jnp
import numpy as np
from jax import lax
from jax.experimental import pallas as pl
from jax.experimental.pallas import tpu as pltpu
from jax.sharding import PartitionSpec as P

PERIODS = 44
DAMPING = 0.05
ROWS = 48
STEP = 32
PTS = 128
ROW_LANE = 64
RUP_LANE = 96
F32 = jnp.float32
BF16 = jnp.bfloat16


def nn(a, b):
    return lax.dot_general(a, b, (((1,), (0,)), ((), ())), preferred_element_type=F32)


def nt(a, b):
    return lax.dot_general(a, b, (((1,), (1,)), ((), ())), preferred_element_type=F32)


def iota(shape, dim):
    return lax.broadcasted_iota(jnp.int32, shape, dim)


def hilo(x):
    hi = x.astype(BF16)
    return hi, (x - hi.astype(F32)).astype(BF16)


def angle(product, n_time):
    return (2.0 * math.pi / n_time) * (product % n_time)


def forward_bases(n_time):
    half = n_time // 2
    quarter = half // 2
    bases = []
    for odd in range(2):
        freq = 2 * np.arange(quarter) + odd
        coarse = angle(np.arange(half // STEP)[:, None] * STEP * freq[None, :], n_time)
        fine = angle(np.arange(STEP)[:, None] * freq[None, :], n_time)
        bases.append(
            np.concatenate([f(x) for x in (coarse, fine) for f in (np.cos, np.sin)]).astype(np.float32)
        )
    return bases


def inverse_bases(n_time):
    half = n_time // 2
    quarter = half // 2
    time = np.arange(half)
    coarse = angle(np.arange(quarter // STEP)[:, None] * 2 * STEP * time[None, :], n_time)
    even = angle(np.arange(STEP)[:, None] * 2 * time[None, :], n_time)
    odd = angle((np.arange(STEP)[:, None] * 2 + 1) * time[None, :], n_time)
    return [
        np.concatenate([f(x) for x in (coarse, fine) for f in (np.cos, np.sin)]).astype(np.float32)
        for fine in (even, odd)
    ]


def ordered(stages, apart):
    place = jnp.zeros_like(apart["worker"])
    for axis, radix, shift, _ in stages:
        place = place * radix + ((apart[axis] >> shift) & (radix - 1))
    return place


def pack_kernel(*refs):
    sources = refs[:4]
    out_ref, scr, own_ref, pts_ref, mom_ref, slip_ref, sems = refs[4:]
    copies = [
        pltpu.make_async_copy(src, dst, sems.at[i])
        for i, (src, dst) in enumerate(zip(sources, (own_ref, pts_ref, mom_ref, slip_ref)))
    ]
    for copy in copies:
        copy.start()
    devices, capacity, _ = out_ref.shape
    slots = devices * capacity
    rup_w, sub = pts_ref.shape
    asked = rup_w * sub
    n_slip = slip_ref.shape[2]
    earlier = (iota((asked, asked), 0) < iota((asked, asked), 1)).astype(F32).astype(BF16)
    spread = iota((128, 6), 0)
    comp = iota((128, 6), 1)
    spread_hi = (spread == comp).astype(F32).astype(BF16)
    spread_lo = (spread == comp + 6).astype(F32).astype(BF16)
    for copy in copies:
        copy.wait()
    own = own_ref[...]
    blocks = own.shape[0]
    both = jnp.concatenate([own // PTS, own % PTS], axis=0).astype(F32).astype(BF16)
    p = jnp.concatenate([pts_ref[r : r + 1, :] for r in range(rup_w)], axis=1)
    in_lane = (iota((128, asked), 0) == p % 128).astype(F32).astype(BF16)
    found = nn(both, in_lane)
    in_block = (iota((blocks, asked), 0) == p // 128).astype(F32)
    dev = jnp.sum(found[:blocks] * in_block, axis=0, keepdims=True)
    loc = jnp.sum(found[blocks:] * in_block, axis=0, keepdims=True)
    onehot = (iota((devices, asked), 0).astype(F32) == dev).astype(F32)
    before = nn(onehot.astype(BF16), earlier)
    rank = jnp.sum(before * onehot, axis=0, keepdims=True)
    target = dev * capacity + rank
    pick = (iota((slots, asked), 0).astype(F32) == target).astype(F32)
    pick16 = pick.astype(BF16)
    mom = jnp.concatenate(
        [
            jnp.concatenate([mom_ref[m, r : r + 1, :] for r in range(rup_w)], axis=1)
            for m in range(6)
        ],
        axis=0,
    )
    hi, lo = hilo(mom)
    rup = (iota((1, asked), 1) // sub).astype(F32)
    lane = iota((128, asked), 0)
    expanded = nn(spread_hi, hi) + nn(spread_lo, lo)
    expanded = jnp.where(lane == ROW_LANE, loc, jnp.where(lane == RUP_LANE, rup, expanded))
    scr[:, n_slip:] = nt(pick16, expanded.astype(BF16))
    slip = slip_ref[...].astype(F32).reshape(asked, n_slip).astype(BF16)
    scr[:, :n_slip] = nn(pick16, slip)
    for d in range(devices):
        out_ref[d] = scr[d * capacity : (d + 1) * capacity, :].astype(BF16)


def owner_kernel(stages, rec_ref, sgt_ref, even_ref, odd_ref, *refs):
    first = stages[0][1]
    out_refs = refs[:first]
    rec_s, x_s, sgt_s, tab_s, sems = refs[first:]
    devices, capacity, width = rec_ref.shape
    slots = devices * capacity
    n_time = sgt_ref.shape[2]
    half = n_time // 2
    quarter = half // 2
    n_slip = width - 128
    wide = 512
    copies = []
    for c in range(3):
        at = slice(6 * c, 6 * c + 6)
        copies.append(pltpu.make_async_copy(sgt_ref.at[at], sgt_s.at[at], sems.at[c]))
    for q, ref in enumerate((even_ref, odd_ref)):
        copies.append(pltpu.make_async_copy(ref, tab_s.at[q], sems.at[3 + q]))
    for copy in copies:
        copy.start()
    for d in range(devices):
        rec_s[d * capacity : (d + 1) * capacity, :] = rec_ref[d].astype(F32)
    tail = rec_s[:, n_slip:]
    row = tail[:, ROW_LANE : ROW_LANE + 1]
    here = iota((slots, PTS), 1).astype(F32) == row
    left = jnp.concatenate(
        [
            jnp.concatenate(
                [jnp.where(here, tail[:, 6 * p + m : 6 * p + m + 1], 0.0).astype(BF16) for m in range(6)],
                axis=1,
            )
            for p in range(2)
        ],
        axis=0,
    )
    for c in range(3):
        copies[c].wait()
        for at in range(0, half, wide):
            ends = []
            for start in (at, half + at):
                rows = sgt_s[6 * c : 6 * c + 6, :, start : start + wide].reshape(6 * PTS, wide)
                out = nn(left, rows)
                ends.append(out[:slots] + out[slots:])
            x_s[c, 0, :, at : at + wide] = (ends[0] + ends[1]).astype(BF16)
            x_s[c, 1, :, at : at + wide] = (ends[0] - ends[1]).astype(BF16)

    ruptures = math.prod(radix for _, radix, _, _ in stages)
    shape = (ruptures, slots)
    rup = nt((iota((8, 128), 1) == RUP_LANE).astype(F32).astype(BF16), tail.astype(BF16))[:1].astype(jnp.int32)
    worker = (iota((1, slots), 1) // capacity) % lax.axis_size("worker")
    apart = {"worker": worker ^ lax.axis_index("worker"), "server": rup ^ lax.axis_index("server")}
    where_to = ordered(stages, apart)
    seg = (iota(shape, 0) == where_to).astype(F32).astype(BF16)
    seg = jnp.concatenate([seg, seg], axis=1)
    slip = rec_s[:, :n_slip].astype(BF16)
    part = ruptures // first
    for q in range(2):
        re = slice(q * quarter, (q + 1) * quarter)
        im = slice(half + q * quarter, half + (q + 1) * quarter)
        copies[3 + q].wait()
        slip_re = nn(slip, tab_s[q, :n_slip, :quarter])
        slip_im = nn(slip, tab_s[q, :n_slip, quarter:])
        for c in range(3):
            x = x_s[c, q]
            t_re = nn(x, tab_s[q, :, :quarter])
            t_im = nn(x, tab_s[q, :, quarter:])
            for cols, prod in (
                (re, slip_re * t_re - slip_im * t_im),
                (im, slip_re * t_im + slip_im * t_re),
            ):
                total = nn(seg, jnp.concatenate(hilo(prod), axis=0))
                for k in range(first):
                    ref = out_refs[k]
                    ref[c, :, cols] = total[k * part : (k + 1) * part].astype(ref.dtype)


def sum_kernel(radix, *refs):
    own_ref = refs[0]
    out_refs = refs[-radix:]
    part = out_refs[0].shape[1]
    for c in range(3):
        total = own_ref[c]
        for ref in refs[1:-radix]:
            total = total + ref[c].astype(F32)
        for k in range(radix):
            out_refs[k][c] = total[k * part : (k + 1) * part].astype(out_refs[k].dtype)


def forward_table_kernel(base_ref, tab_ref):
    half = tab_ref.shape[0]
    quarter = half // 2
    count = half // STEP
    wide = 256
    for lc in range(quarter // wide):
        sl = slice(lc * wide, (lc + 1) * wide)
        sl2 = slice(quarter + lc * wide, quarter + (lc + 1) * wide)
        cb = base_ref[2 * count : 2 * count + STEP, sl]
        sb = base_ref[2 * count + STEP :, sl]

        def table(a, carry):
            ca = base_ref[pl.ds(a, 1), sl]
            sa = base_ref[pl.ds(count + a, 1), sl]
            at = pl.ds(pl.multiple_of(a * STEP, STEP), STEP)
            tab_ref[at, sl] = (ca * cb - sa * sb).astype(BF16)
            tab_ref[at, sl2] = (-(sa * cb + ca * sb)).astype(BF16)
            return carry

        lax.fori_loop(0, count, table, 0)


def inverse_table_kernel(base_ref, hi_ref, lo_ref):
    half = hi_ref.shape[0]
    quarter = half // 2
    count = quarter // STEP
    wide = 256
    for lc in range(half // wide):
        sl = slice(lc * wide, (lc + 1) * wide)
        cf = base_ref[2 * count : 2 * count + STEP, sl]
        sf = base_ref[2 * count + STEP :, sl]

        def table(a, carry):
            ca = base_ref[pl.ds(a, 1), sl]
            sa = base_ref[pl.ds(count + a, 1), sl]
            for base, value in ((0, ca * cf - sa * sf), (quarter, -(sa * cf + ca * sf))):
                at = pl.ds(pl.multiple_of(base + a * STEP, STEP), STEP)
                hi, lo = hilo(value)
                hi_ref[at, sl] = hi
                lo_ref[at, sl] = lo
            return carry

        lax.fori_loop(0, count, table, 0)


def gain_kernel(gr_ref, gi_ref):
    half = gr_ref.shape[1]
    quarter = half // 2
    n_time = 2 * half
    shape = gr_ref.shape
    low = math.log(4.0 / n_time)
    high = math.log(0.25)
    period = iota(shape, 0)
    slot = iota(shape, 1)
    freq = jnp.where(slot < quarter, 2 * slot, 2 * (slot - quarter) + 1)
    omega_freq = freq.astype(F32) * (2.0 * math.pi / n_time)
    omega_osc = 2.0 * math.pi * jnp.exp(low + (high - low) * period.astype(F32) / (PERIODS - 1))
    den_real = omega_osc * omega_osc - omega_freq * omega_freq
    den_imag = 2.0 * DAMPING * omega_osc * omega_freq
    weight = jnp.where(freq == 0, 1.0, 2.0) / n_time
    gain = weight * (omega_osc * omega_osc / (den_real * den_real + den_imag * den_imag))
    gr_ref[...] = jnp.where(period < PERIODS, -gain * den_real, weight)
    gi_ref[...] = jnp.where(period < PERIODS, -gain * den_imag, 0.0)


def final_kernel(count, *refs):
    spec_refs = refs[:count]
    *tables, gr_ref, gi_ref, seis_ref, peak_ref = refs[count:]
    half = gr_ref.shape[1]
    quarter = half // 2
    spec = []
    for c in range(3):
        total = spec_refs[0][c]
        for ref in spec_refs[1:]:
            total = total + ref[c].astype(F32)
        spec.append(total)
    gr = gr_ref[...]
    gi = gi_ref[...]
    sums = []
    for q in range(2):
        cols = slice(q * quarter, (q + 1) * quarter)
        cols_im = slice(half + q * quarter, half + (q + 1) * quarter)
        lefts = []
        for c in range(3):
            re = spec[c][:, cols]
            im = spec[c][:, cols_im]
            g_re = gr[:, cols]
            g_im = gi[:, cols]
            lefts.append(jnp.concatenate([re * g_re + im * g_im, im * g_re - re * g_im], axis=1))
        hi, lo = hilo(jnp.concatenate(lefts, axis=0))
        hi_ref, lo_ref = tables[2 * q : 2 * q + 2]
        first = nn(jnp.concatenate([hi, lo], axis=0), hi_ref[...])
        sums.append(first[: 3 * ROWS] + first[3 * ROWS :] + nn(hi, lo_ref[...]))
    even, odd = sums
    peak = jnp.max(jnp.abs(even) + jnp.abs(odd), axis=1, keepdims=True)
    for c in range(3):
        row = c * ROWS + PERIODS
        seis_ref[c, :, :half] = even[row : row + 1] + odd[row : row + 1]
        seis_ref[c, :, half:] = even[row : row + 1] - odd[row : row + 1]
        column = jnp.broadcast_to(peak[c * ROWS : (c + 1) * ROWS], (ROWS, 128))
        column = jnp.concatenate([column, jnp.zeros((128 - ROWS, 128), F32)], axis=0)
        peak_ref[c] = column.T[:1, :PERIODS]


def vmem():
    return pl.BlockSpec(memory_space=pltpu.VMEM)


def hbm():
    return pl.BlockSpec(memory_space=pltpu.HBM)


def in_hbm(x):
    return pltpu.with_memory_space_constraint(x, pltpu.HBM)


def params(mib):
    return pltpu.CompilerParams(vmem_limit_bytes=mib << 20)


def exchange_plan(n_worker, n_server):
    stages = []
    for axis, size in (("worker", n_worker), ("server", n_server)):
        bits = size.bit_length() - 1
        assert size == 1 << bits
        shift = 0
        while shift < bits:
            step = 1 if (bits - shift) % 2 else 2
            stages.append((axis, 1 << step, shift, size))
            shift += step
    return stages


def send(parts, stage):
    axis, radix, shift, size = stage
    return [
        lax.ppermute(parts[k], axis, [(i, i ^ (k << shift)) for i in range(size)])
        for k in range(radix - 1, 0, -1)
    ]


def beside(kernel, base, own):
    base, own = lax.optimization_barrier((jnp.asarray(base), own))
    own, *made = lax.optimization_barrier((own, *kernel(base)))
    return own, made


def sent_type(stages, i):
    return F32 if i == 0 or i == len(stages) - 1 else BF16


def shards(n_server, n_worker, sgt, ownership, sub_points, moments, slip):
    devices = n_server * n_worker
    n_time = sgt.shape[2]
    half = n_time // 2
    rup_w = sub_points.shape[1]
    sub_dev = sub_points.shape[2]
    n_slip = slip.shape[3]
    capacity = 4 * sub_dev // (3 * n_worker)
    slots = devices * capacity
    width = n_slip + 128
    stages = exchange_plan(n_worker, n_server)
    assert rup_w == n_server and sgt.shape[0] == PTS and slots % 16 == 0

    forward = pl.pallas_call(
        forward_table_kernel,
        out_shape=[jax.ShapeDtypeStruct((half, half), BF16)],
        in_specs=[vmem()],
        out_specs=[vmem()],
        compiler_params=params(4),
        cost_estimate=pl.CostEstimate(flops=10**9, bytes_accessed=10**7, transcendentals=0),
        name="forward_table",
    )

    record = pl.pallas_call(
        pack_kernel,
        out_shape=jax.ShapeDtypeStruct((devices, capacity, width), BF16),
        in_specs=[hbm()] * 4,
        out_specs=vmem(),
        scratch_shapes=[
            pltpu.VMEM((slots, width), F32),
            pltpu.VMEM((ownership.shape[0] // 128, 128), jnp.int32),
            pltpu.VMEM((rup_w, sub_dev), jnp.int32),
            pltpu.VMEM((6, rup_w, sub_dev), F32),
            pltpu.VMEM((rup_w, sub_dev, n_slip), BF16),
            pltpu.SemaphoreType.DMA((4,)),
        ],
        compiler_params=params(12),
        name="pack",
    )(
        *[
            in_hbm(x)
            for x in (
                ownership.reshape(-1, 128),
                sub_points[0],
                jnp.transpose(moments[0], (1, 0, 2)),
                slip[0],
            )
        ]
    )
    record = lax.all_to_all(record, ("server", "worker"), split_axis=0, concat_axis=0, tiled=True)
    forwards = [in_hbm(forward(jnp.asarray(base))[0]) for base in forward_bases(n_time)]

    inverse = pl.pallas_call(
        inverse_table_kernel,
        out_shape=[jax.ShapeDtypeStruct((half, half), BF16)] * 2,
        in_specs=[vmem()],
        out_specs=[vmem()] * 2,
        compiler_params=params(8),
        cost_estimate=pl.CostEstimate(flops=10**9, bytes_accessed=10**7, transcendentals=0),
        name="inverse_table",
    )
    gain = pl.pallas_call(
        gain_kernel,
        out_shape=[jax.ShapeDtypeStruct((ROWS, half), F32)] * 2,
        out_specs=[vmem()] * 2,
        compiler_params=params(2),
        name="gain",
    )()
    tables = []
    bases = inverse_bases(n_time)

    def part_shapes(i):
        count = math.prod(radix for _, radix, _, _ in stages[i + 1 :])
        return [
            jax.ShapeDtypeStruct((3, count, n_time), sent_type(stages, i) if k else F32)
            for k in range(stages[i][1])
        ]

    parts = pl.pallas_call(
        functools.partial(owner_kernel, stages),
        out_shape=part_shapes(0),
        in_specs=[vmem()] + [hbm()] * 3,
        out_specs=[vmem()] * stages[0][1],
        scratch_shapes=[
            pltpu.VMEM((slots, width), F32),
            pltpu.VMEM((3, 2, slots, half), BF16),
            pltpu.VMEM((18, PTS, n_time), BF16),
            pltpu.VMEM((2, half, half), BF16),
            pltpu.SemaphoreType.DMA((5,)),
        ],
        compiler_params=params(36),
        cost_estimate=pl.CostEstimate(flops=10**10, bytes_accessed=2 * 10**7, transcendentals=0),
        name="owner",
    )(record, in_hbm(jnp.transpose(sgt, (1, 0, 2))), *forwards)
    arrived = send(parts, stages[0])
    for i in range(1, len(stages)):
        radix = stages[i][1]
        parts = pl.pallas_call(
            functools.partial(sum_kernel, radix),
            out_shape=part_shapes(i),
            in_specs=[vmem()] * (1 + len(arrived)),
            out_specs=[vmem()] * radix,
            compiler_params=params(4),
            name=f"sum_{i}",
        )(parts[0], *arrived)
        arrived = send(parts, stages[i])
        if i >= len(stages) - 2:
            own, pair = beside(inverse, bases[len(tables) // 2], parts[0])
            parts = [own]
            tables += pair
    count = 1 + len(arrived)
    seis, peaks = pl.pallas_call(
        functools.partial(final_kernel, count),
        out_shape=[
            jax.ShapeDtypeStruct((3, 1, n_time), F32),
            jax.ShapeDtypeStruct((3, 1, PERIODS), F32),
        ],
        in_specs=[vmem()] * (count + 6),
        out_specs=[vmem()] * 2,
        compiler_params=params(20),
        name="finish",
    )(parts[0], *arrived, *tables, *gain)
    return (
        jnp.transpose(seis, (1, 0, 2)).reshape(1, 1, 3, n_time),
        jnp.transpose(peaks, (1, 0, 2)).reshape(1, 1, 3, PERIODS),
    )


def solution(mesh):
    placed = (
        P(("server", "worker"), None, None),
        P(),
        P("worker", None, "server"),
        P("worker", None, None, "server"),
        P("worker", None, "server", None),
    )
    return jax.shard_map(
        functools.partial(shards, mesh.shape["server"], mesh.shape["worker"]),
        mesh=mesh,
        in_specs=placed,
        out_specs=(P("worker", "server", None, None), P("worker", "server", None, None)),
        check_vma=False,
    )
```

```python
import functools
import math

import jax
import jax.numpy as jnp
import numpy as np
from jax import lax
from jax.experimental import pallas as pl
from jax.experimental.pallas import tpu as pltpu
from jax.sharding import PartitionSpec as P

PERIODS = 44
DAMPING = 0.05
ROWS = 48
STEP = 32
PTS = 128
DFT_WIDE = 512
ROW_LANE = 64
RUP_LANE = 96
F32 = jnp.float32
BF16 = jnp.bfloat16


def nn(a, b):
    return lax.dot_general(a, b, (((1,), (0,)), ((), ())), preferred_element_type=F32)


def nt(a, b):
    return lax.dot_general(a, b, (((1,), (1,)), ((), ())), preferred_element_type=F32)


def iota(shape, dim):
    return lax.broadcasted_iota(jnp.int32, shape, dim)


def hilo(x):
    hi = x.astype(BF16)
    return hi, (x - hi.astype(F32)).astype(BF16)


def angle(product, n_time):
    return (2.0 * math.pi / n_time) * (product % n_time)


def forward_bases(n_time):
    half = n_time // 2
    quarter = half // 2
    bases = []
    for odd in range(2):
        freq = 2 * np.arange(quarter) + odd
        coarse = angle(np.arange(half // STEP)[:, None] * STEP * freq[None, :], n_time)
        fine = angle(np.arange(STEP)[:, None] * freq[None, :], n_time)
        bases.append(
            np.concatenate([f(x) for x in (coarse, fine) for f in (np.cos, np.sin)]).astype(np.float32)
        )
    return bases


def inverse_bases(n_time):
    half = n_time // 2
    quarter = half // 2
    time = np.arange(half)
    coarse = angle(np.arange(quarter // STEP)[:, None] * 2 * STEP * time[None, :], n_time)
    even = angle(np.arange(STEP)[:, None] * 2 * time[None, :], n_time)
    odd = angle((np.arange(STEP)[:, None] * 2 + 1) * time[None, :], n_time)
    return [
        np.concatenate([f(x) for x in (coarse, fine) for f in (np.cos, np.sin)]).astype(np.float32)
        for fine in (even, odd)
    ]


def ordered(stages, apart):
    place = jnp.zeros_like(apart["worker"])
    for axis, radix, shift, _ in stages:
        place = place * radix + ((apart[axis] >> shift) & (radix - 1))
    return place


def pack_kernel(*refs):
    sources = refs[:4]
    out_ref, scr, own_ref, pts_ref, mom_ref, slip_ref, sems = refs[4:]
    copies = [
        pltpu.make_async_copy(src, dst, sems.at[i])
        for i, (src, dst) in enumerate(zip(sources, (own_ref, pts_ref, mom_ref, slip_ref)))
    ]
    for copy in copies:
        copy.start()
    devices, capacity, _ = out_ref.shape
    slots = devices * capacity
    rup_w, sub = pts_ref.shape
    asked = rup_w * sub
    n_slip = slip_ref.shape[2]
    earlier = (iota((asked, asked), 0) < iota((asked, asked), 1)).astype(F32).astype(BF16)
    spread = iota((128, 6), 0)
    comp = iota((128, 6), 1)
    spread_hi = (spread == comp).astype(F32).astype(BF16)
    spread_lo = (spread == comp + 6).astype(F32).astype(BF16)
    for copy in copies:
        copy.wait()
    own = own_ref[...]
    blocks = own.shape[0]
    both = jnp.concatenate([own // PTS, own % PTS], axis=0).astype(F32).astype(BF16)
    p = jnp.concatenate([pts_ref[r : r + 1, :] for r in range(rup_w)], axis=1)
    in_lane = (iota((128, asked), 0) == p % 128).astype(F32).astype(BF16)
    found = nn(both, in_lane)
    in_block = (iota((blocks, asked), 0) == p // 128).astype(F32)
    dev = jnp.sum(found[:blocks] * in_block, axis=0, keepdims=True)
    loc = jnp.sum(found[blocks:] * in_block, axis=0, keepdims=True)
    onehot = (iota((devices, asked), 0).astype(F32) == dev).astype(F32)
    before = nn(onehot.astype(BF16), earlier)
    rank = jnp.sum(before * onehot, axis=0, keepdims=True)
    target = dev * capacity + rank
    pick = (iota((slots, asked), 0).astype(F32) == target).astype(F32)
    pick16 = pick.astype(BF16)
    mom = jnp.concatenate(
        [
            jnp.concatenate([mom_ref[m, r : r + 1, :] for r in range(rup_w)], axis=1)
            for m in range(6)
        ],
        axis=0,
    )
    hi, lo = hilo(mom)
    rup = (iota((1, asked), 1) // sub).astype(F32)
    lane = iota((128, asked), 0)
    expanded = nn(spread_hi, hi) + nn(spread_lo, lo)
    expanded = jnp.where(lane == ROW_LANE, loc, jnp.where(lane == RUP_LANE, rup, expanded))
    scr[:, n_slip:] = nt(pick16, expanded.astype(BF16))
    slip = slip_ref[...].astype(F32).reshape(asked, n_slip).astype(BF16)
    scr[:, :n_slip] = nn(pick16, slip)
    for d in range(devices):
        out_ref[d] = scr[d * capacity : (d + 1) * capacity, :].astype(BF16)


def forward_table(base_ref, tab_ref):
    half, width = tab_ref.shape
    quarter = width // 2
    count = half // STEP
    wide = 256
    for lc in range(quarter // wide):
        sl = slice(lc * wide, (lc + 1) * wide)
        sl2 = slice(quarter + lc * wide, quarter + (lc + 1) * wide)
        cb = base_ref[2 * count : 2 * count + STEP, sl]
        sb = base_ref[2 * count + STEP :, sl]

        def table(a, carry):
            ca = base_ref[pl.ds(a, 1), sl]
            sa = base_ref[pl.ds(count + a, 1), sl]
            at = pl.ds(pl.multiple_of(a * STEP, STEP), STEP)
            tab_ref[at, sl] = (ca * cb - sa * sb).astype(BF16)
            tab_ref[at, sl2] = (-(sa * cb + ca * sb)).astype(BF16)
            return carry

        lax.fori_loop(0, count, table, 0, unroll=4)


def owner_kernel(stages, rec_ref, sgt_ref, base_ref, *refs):
    first = stages[0][1]
    out_refs = refs[:first]
    rec_s, x_s, sgt_s, base_s, tab_s, sems = refs[first:]
    devices, capacity, width = rec_ref.shape
    slots = devices * capacity
    n_time = sgt_ref.shape[2]
    half = n_time // 2
    quarter = half // 2
    n_slip = width - 128
    wide = 512
    base_copy = pltpu.make_async_copy(base_ref, base_s, sems.at[3])
    base_copy.start()
    copies = []
    for c in range(3):
        at = slice(6 * c, 6 * c + 6)
        copies.append(pltpu.make_async_copy(sgt_ref.at[at], sgt_s.at[at], sems.at[c]))
        copies[c].start()
    for d in range(devices):
        rec_s[d * capacity : (d + 1) * capacity, :] = rec_ref[d].astype(F32)
    tail = rec_s[:, n_slip:]
    row = tail[:, ROW_LANE : ROW_LANE + 1]
    here = iota((slots, PTS), 1).astype(F32) == row
    left = jnp.concatenate(
        [
            jnp.concatenate(
                [jnp.where(here, tail[:, 6 * p + m : 6 * p + m + 1], 0.0).astype(BF16) for m in range(6)],
                axis=1,
            )
            for p in range(2)
        ],
        axis=0,
    )
    base_copy.wait()
    for c in range(3):
        if c < 2:
            forward_table(base_s.at[c], tab_s.at[c])
        copies[c].wait()
        for at in range(0, half, wide):
            ends = []
            for start in (at, half + at):
                rows = sgt_s[6 * c : 6 * c + 6, :, start : start + wide].reshape(6 * PTS, wide)
                out = nn(left, rows)
                ends.append(out[:slots] + out[slots:])
            x_s[0, c * slots : (c + 1) * slots, at : at + wide] = (ends[0] + ends[1]).astype(BF16)
            x_s[1, c * slots : (c + 1) * slots, at : at + wide] = (ends[0] - ends[1]).astype(BF16)

    ruptures = math.prod(radix for _, radix, _, _ in stages)
    shape = (ruptures, slots)
    rup = nt((iota((8, 128), 1) == RUP_LANE).astype(F32).astype(BF16), tail.astype(BF16))[:1].astype(jnp.int32)
    worker = (iota((1, slots), 1) // capacity) % lax.axis_size("worker")
    apart = {"worker": worker ^ lax.axis_index("worker"), "server": rup ^ lax.axis_index("server")}
    where_to = ordered(stages, apart)
    seg = (iota(shape, 0) == where_to).astype(F32).astype(BF16)
    seg = jnp.concatenate([seg, seg], axis=1)
    slip = rec_s[:, :n_slip].astype(BF16)
    part = ruptures // first
    for q in range(2):
        for at in range(0, quarter, DFT_WIDE):
            cols = slice(at, at + DFT_WIDE)
            cols_im = slice(quarter + at, quarter + at + DFT_WIDE)
            slip_re = nn(slip, tab_s[q, :n_slip, cols])
            slip_im = nn(slip, tab_s[q, :n_slip, cols_im])
            all_re = nn(x_s[q], tab_s[q, :, cols])
            all_im = nn(x_s[q], tab_s[q, :, cols_im])
            for c in range(3):
                t_re = all_re[c * slots : (c + 1) * slots]
                t_im = all_im[c * slots : (c + 1) * slots]
                for base, prod in (
                    (0, slip_re * t_re - slip_im * t_im),
                    (half, slip_re * t_im + slip_im * t_re),
                ):
                    start = base + q * quarter + at
                    total = nn(seg, jnp.concatenate(hilo(prod), axis=0))
                    for k in range(first):
                        ref = out_refs[k]
                        ref[c, :, start : start + DFT_WIDE] = total[k * part : (k + 1) * part].astype(ref.dtype)


def sum_kernel(radix, *refs):
    own_ref = refs[0]
    out_refs = refs[-radix:]
    part = out_refs[0].shape[1]
    for c in range(3):
        total = own_ref[c]
        for ref in refs[1:-radix]:
            total = total + ref[c].astype(F32)
        for k in range(radix):
            out_refs[k][c] = total[k * part : (k + 1) * part].astype(out_refs[k].dtype)


def inverse_table_kernel(base_ref, hi_ref, lo_ref):
    half = hi_ref.shape[0]
    quarter = half // 2
    count = quarter // STEP
    wide = 256
    for lc in range(half // wide):
        sl = slice(lc * wide, (lc + 1) * wide)
        cf = base_ref[2 * count : 2 * count + STEP, sl]
        sf = base_ref[2 * count + STEP :, sl]

        def table(a, carry):
            ca = base_ref[pl.ds(a, 1), sl]
            sa = base_ref[pl.ds(count + a, 1), sl]
            for base, value in ((0, ca * cf - sa * sf), (quarter, -(sa * cf + ca * sf))):
                at = pl.ds(pl.multiple_of(base + a * STEP, STEP), STEP)
                hi, lo = hilo(value)
                hi_ref[at, sl] = hi
                lo_ref[at, sl] = lo
            return carry

        lax.fori_loop(0, count, table, 0)


def gain_kernel(gr_ref, gi_ref):
    half = gr_ref.shape[1]
    quarter = half // 2
    n_time = 2 * half
    shape = gr_ref.shape
    low = math.log(4.0 / n_time)
    high = math.log(0.25)
    period = iota(shape, 0)
    slot = iota(shape, 1)
    freq = jnp.where(slot < quarter, 2 * slot, 2 * (slot - quarter) + 1)
    omega_freq = freq.astype(F32) * (2.0 * math.pi / n_time)
    omega_osc = 2.0 * math.pi * jnp.exp(low + (high - low) * period.astype(F32) / (PERIODS - 1))
    den_real = omega_osc * omega_osc - omega_freq * omega_freq
    den_imag = 2.0 * DAMPING * omega_osc * omega_freq
    weight = jnp.where(freq == 0, 1.0, 2.0) / n_time
    gain = weight * (omega_osc * omega_osc / (den_real * den_real + den_imag * den_imag))
    gr_ref[...] = jnp.where(period < PERIODS, -gain * den_real, weight)
    gi_ref[...] = jnp.where(period < PERIODS, -gain * den_imag, 0.0)


def final_kernel(count, *refs):
    spec_refs = refs[:count]
    *tables, gr_ref, gi_ref, seis_ref, peak_ref = refs[count:]
    half = gr_ref.shape[1]
    quarter = half // 2
    spec = []
    for c in range(3):
        total = spec_refs[0][c]
        for ref in spec_refs[1:]:
            total = total + ref[c].astype(F32)
        spec.append(total)
    gr = gr_ref[...]
    gi = gi_ref[...]
    sums = []
    for q in range(2):
        cols = slice(q * quarter, (q + 1) * quarter)
        cols_im = slice(half + q * quarter, half + (q + 1) * quarter)
        lefts = []
        for c in range(3):
            re = spec[c][:, cols]
            im = spec[c][:, cols_im]
            g_re = gr[:, cols]
            g_im = gi[:, cols]
            lefts.append(jnp.concatenate([re * g_re + im * g_im, im * g_re - re * g_im], axis=1))
        hi, lo = hilo(jnp.concatenate(lefts, axis=0))
        hi_ref, lo_ref = tables[2 * q : 2 * q + 2]
        first = nn(jnp.concatenate([hi, lo], axis=0), hi_ref[...])
        sums.append(first[: 3 * ROWS] + first[3 * ROWS :] + nn(hi, lo_ref[...]))
    even, odd = sums
    peak = jnp.max(jnp.abs(even) + jnp.abs(odd), axis=1, keepdims=True)
    for c in range(3):
        row = c * ROWS + PERIODS
        seis_ref[c, :, :half] = even[row : row + 1] + odd[row : row + 1]
        seis_ref[c, :, half:] = even[row : row + 1] - odd[row : row + 1]
        column = jnp.broadcast_to(peak[c * ROWS : (c + 1) * ROWS], (ROWS, 128))
        column = jnp.concatenate([column, jnp.zeros((128 - ROWS, 128), F32)], axis=0)
        peak_ref[c] = column.T[:1, :PERIODS]


def vmem():
    return pl.BlockSpec(memory_space=pltpu.VMEM)


def hbm():
    return pl.BlockSpec(memory_space=pltpu.HBM)


def in_hbm(x):
    return pltpu.with_memory_space_constraint(x, pltpu.HBM)


def params(mib):
    return pltpu.CompilerParams(vmem_limit_bytes=mib << 20)


def exchange_plan(n_worker, n_server):
    stages = []
    for axis, size in (("worker", n_worker), ("server", n_server)):
        bits = size.bit_length() - 1
        assert size == 1 << bits
        shift = 0
        while shift < bits:
            step = 1 if (bits - shift) % 2 else 2
            stages.append((axis, 1 << step, shift, size))
            shift += step
    return stages


def send(parts, stage):
    axis, radix, shift, size = stage
    return [
        lax.ppermute(parts[k], axis, [(i, i ^ (k << shift)) for i in range(size)])
        for k in range(radix - 1, 0, -1)
    ]


def beside(kernel, base, own):
    base, own = lax.optimization_barrier((jnp.asarray(base), own))
    own, *made = lax.optimization_barrier((own, *kernel(base)))
    return own, made


def sent_type(stages, i):
    return F32 if i == 0 or i == len(stages) - 1 else BF16


def shards(n_server, n_worker, sgt, ownership, sub_points, moments, slip):
    devices = n_server * n_worker
    n_time = sgt.shape[2]
    half = n_time // 2
    rup_w = sub_points.shape[1]
    sub_dev = sub_points.shape[2]
    n_slip = slip.shape[3]
    capacity = 4 * sub_dev // (3 * n_worker)
    slots = devices * capacity
    width = n_slip + 128
    stages = exchange_plan(n_worker, n_server)
    assert rup_w == n_server and sgt.shape[0] == PTS and slots % 16 == 0

    record = pl.pallas_call(
        pack_kernel,
        out_shape=jax.ShapeDtypeStruct((devices, capacity, width), BF16),
        in_specs=[hbm()] * 4,
        out_specs=vmem(),
        scratch_shapes=[
            pltpu.VMEM((slots, width), F32),
            pltpu.VMEM((ownership.shape[0] // 128, 128), jnp.int32),
            pltpu.VMEM((rup_w, sub_dev), jnp.int32),
            pltpu.VMEM((6, rup_w, sub_dev), F32),
            pltpu.VMEM((rup_w, sub_dev, n_slip), BF16),
            pltpu.SemaphoreType.DMA((4,)),
        ],
        compiler_params=params(12),
        name="pack",
    )(
        *[
            in_hbm(x)
            for x in (
                ownership.reshape(-1, 128),
                sub_points[0],
                jnp.transpose(moments[0], (1, 0, 2)),
                slip[0],
            )
        ]
    )
    record = lax.all_to_all(record, ("server", "worker"), split_axis=0, concat_axis=0, tiled=True)
    base = jnp.asarray(np.stack(forward_bases(n_time)))

    inverse = pl.pallas_call(
        inverse_table_kernel,
        out_shape=[jax.ShapeDtypeStruct((half, half), BF16)] * 2,
        in_specs=[vmem()],
        out_specs=[vmem()] * 2,
        compiler_params=params(8),
        cost_estimate=pl.CostEstimate(flops=10**9, bytes_accessed=10**7, transcendentals=0),
        name="inverse_table",
    )
    gain = pl.pallas_call(
        gain_kernel,
        out_shape=[jax.ShapeDtypeStruct((ROWS, half), F32)] * 2,
        out_specs=[vmem()] * 2,
        compiler_params=params(2),
        name="gain",
    )()
    tables = []
    bases = inverse_bases(n_time)

    def part_shapes(i):
        count = math.prod(radix for _, radix, _, _ in stages[i + 1 :])
        return [
            jax.ShapeDtypeStruct((3, count, n_time), sent_type(stages, i) if k else F32)
            for k in range(stages[i][1])
        ]

    parts = pl.pallas_call(
        functools.partial(owner_kernel, stages),
        out_shape=part_shapes(0),
        in_specs=[vmem()] + [hbm()] * 2,
        out_specs=[vmem()] * stages[0][1],
        scratch_shapes=[
            pltpu.VMEM((slots, width), F32),
            pltpu.VMEM((2, 3 * slots, half), BF16),
            pltpu.VMEM((18, PTS, n_time), BF16),
            pltpu.VMEM(base.shape, F32),
            pltpu.VMEM((2, half, half), BF16),
            pltpu.SemaphoreType.DMA((4,)),
        ],
        compiler_params=params(36),
        cost_estimate=pl.CostEstimate(flops=10**10, bytes_accessed=2 * 10**7, transcendentals=0),
        name="owner",
    )(record, in_hbm(jnp.transpose(sgt, (1, 0, 2))), in_hbm(base))
    arrived = send(parts, stages[0])
    for i in range(1, len(stages)):
        radix = stages[i][1]
        parts = pl.pallas_call(
            functools.partial(sum_kernel, radix),
            out_shape=part_shapes(i),
            in_specs=[vmem()] * (1 + len(arrived)),
            out_specs=[vmem()] * radix,
            compiler_params=params(4),
            name=f"sum_{i}",
        )(parts[0], *arrived)
        arrived = send(parts, stages[i])
        if i >= len(stages) - 2:
            own, pair = beside(inverse, bases[len(tables) // 2], parts[0])
            parts = [own]
            tables += pair
    count = 1 + len(arrived)
    seis, peaks = pl.pallas_call(
        functools.partial(final_kernel, count),
        out_shape=[
            jax.ShapeDtypeStruct((3, 1, n_time), F32),
            jax.ShapeDtypeStruct((3, 1, PERIODS), F32),
        ],
        in_specs=[vmem()] * (count + 6),
        out_specs=[vmem()] * 2,
        compiler_params=params(20),
        name="finish",
    )(parts[0], *arrived, *tables, *gain)
    return (
        jnp.transpose(seis, (1, 0, 2)).reshape(1, 1, 3, n_time),
        jnp.transpose(peaks, (1, 0, 2)).reshape(1, 1, 3, PERIODS),
    )


def solution(mesh):
    placed = (
        P(("server", "worker"), None, None),
        P(),
        P("worker", None, "server"),
        P("worker", None, None, "server"),
        P("worker", None, "server", None),
    )
    return jax.shard_map(
        functools.partial(shards, mesh.shape["server"], mesh.shape["worker"]),
        mesh=mesh,
        in_specs=placed,
        out_specs=(P("worker", "server", None, None), P("worker", "server", None, None)),
        check_vma=False,
    )
```

```python
import functools
import math

import jax
import jax.numpy as jnp
import numpy as np
from jax import lax
from jax.experimental import pallas as pl
from jax.experimental.pallas import tpu as pltpu
from jax.sharding import PartitionSpec as P

PERIODS = 44
DAMPING = 0.05
ROWS = 48
STEP = 32
PTS = 128
RESIDUES = (0, 2, 1, 3)
ROW_LANE = 64
RUP_LANE = 96
F32 = jnp.float32
BF16 = jnp.bfloat16


def nn(a, b):
    return lax.dot_general(a, b, (((1,), (0,)), ((), ())), preferred_element_type=F32)


def nt(a, b):
    return lax.dot_general(a, b, (((1,), (1,)), ((), ())), preferred_element_type=F32)


def iota(shape, dim):
    return lax.broadcasted_iota(jnp.int32, shape, dim)


def hilo(x):
    hi = x.astype(BF16)
    return hi, (x - hi.astype(F32)).astype(BF16)


def angle(product, n_time):
    return (2.0 * math.pi / n_time) * (product % n_time)


def cos_sin(*angles):
    return np.concatenate([f(x) for x in angles for f in (np.cos, np.sin)]).astype(np.float32)


def forward_base(n_time):
    index = np.arange(n_time // 8)
    freq = np.concatenate([4 * index + residue for residue in RESIDUES])
    coarse = angle(np.arange(n_time // 4 // STEP)[:, None] * STEP * freq[None, :], n_time)
    fine = angle(np.arange(STEP)[:, None] * freq[None, :], n_time)
    return cos_sin(coarse, fine)


def inverse_bases(n_time):
    time = np.arange(n_time // 4)
    coarse = angle(np.arange(n_time // 8 // STEP)[:, None] * 4 * STEP * time[None, :], n_time)
    fine = [
        angle((np.arange(STEP)[:, None] * 4 + residue) * time[None, :], n_time)
        for residue in RESIDUES
    ]
    return [cos_sin(coarse, *fine[:2]), cos_sin(coarse, *fine[2:])]


def ordered(stages, apart):
    place = jnp.zeros_like(apart["worker"])
    for axis, radix, shift, _ in stages:
        place = place * radix + ((apart[axis] >> shift) & (radix - 1))
    return place


def pack_kernel(*refs):
    sources = refs[:4]
    out_ref, scr, own_ref, pts_ref, mom_ref, slip_ref, sems = refs[4:]
    copies = [
        pltpu.make_async_copy(src, dst, sems.at[i])
        for i, (src, dst) in enumerate(zip(sources, (own_ref, pts_ref, mom_ref, slip_ref)))
    ]
    for copy in copies:
        copy.start()
    devices, capacity, _ = out_ref.shape
    slots = devices * capacity
    rup_w, sub = pts_ref.shape
    asked = rup_w * sub
    n_slip = slip_ref.shape[2]
    earlier = (iota((asked, asked), 0) < iota((asked, asked), 1)).astype(F32).astype(BF16)
    spread = iota((128, 6), 0)
    comp = iota((128, 6), 1)
    spread_hi = (spread == comp).astype(F32).astype(BF16)
    spread_lo = (spread == comp + 6).astype(F32).astype(BF16)
    for copy in copies:
        copy.wait()
    own = own_ref[...]
    blocks = own.shape[0]
    both = jnp.concatenate([own // PTS, own % PTS], axis=0).astype(F32).astype(BF16)
    p = jnp.concatenate([pts_ref[r : r + 1, :] for r in range(rup_w)], axis=1)
    in_lane = (iota((128, asked), 0) == p % 128).astype(F32).astype(BF16)
    found = nn(both, in_lane)
    in_block = (iota((blocks, asked), 0) == p // 128).astype(F32)
    dev = jnp.sum(found[:blocks] * in_block, axis=0, keepdims=True)
    loc = jnp.sum(found[blocks:] * in_block, axis=0, keepdims=True)
    onehot = (iota((devices, asked), 0).astype(F32) == dev).astype(F32)
    before = nn(onehot.astype(BF16), earlier)
    rank = jnp.sum(before * onehot, axis=0, keepdims=True)
    target = dev * capacity + rank
    pick = (iota((slots, asked), 0).astype(F32) == target).astype(F32)
    pick16 = pick.astype(BF16)
    mom = jnp.concatenate(
        [
            jnp.concatenate([mom_ref[m, r : r + 1, :] for r in range(rup_w)], axis=1)
            for m in range(6)
        ],
        axis=0,
    )
    hi, lo = hilo(mom)
    rup = (iota((1, asked), 1) // sub).astype(F32)
    lane = iota((128, asked), 0)
    expanded = nn(spread_hi, hi) + nn(spread_lo, lo)
    expanded = jnp.where(lane == ROW_LANE, loc, jnp.where(lane == RUP_LANE, rup, expanded))
    scr[:, n_slip:] = nt(pick16, expanded.astype(BF16))
    slip = slip_ref[...].astype(F32).reshape(asked, n_slip).astype(BF16)
    scr[:, :n_slip] = nn(pick16, slip)
    for d in range(devices):
        out_ref[d] = scr[d * capacity : (d + 1) * capacity, :].astype(BF16)


def forward_table(base_ref, tab_ref, block):
    count = tab_ref.shape[0] // STEP
    wide = tab_ref.shape[1] // 8
    sl = slice(block * wide, (block + 1) * wide)
    cols = slice(2 * block * wide, (2 * block + 1) * wide)
    cols_im = slice((2 * block + 1) * wide, (2 * block + 2) * wide)
    cb = base_ref[2 * count : 2 * count + STEP, sl]
    sb = base_ref[2 * count + STEP :, sl]

    def table(a, carry):
        ca = base_ref[pl.ds(a, 1), sl]
        sa = base_ref[pl.ds(count + a, 1), sl]
        at = pl.ds(pl.multiple_of(a * STEP, STEP), STEP)
        tab_ref[at, cols] = (ca * cb - sa * sb).astype(BF16)
        tab_ref[at, cols_im] = (-(sa * cb + ca * sb)).astype(BF16)
        return carry

    lax.fori_loop(0, count, table, 0, unroll=4)


def owner_kernel(stages, rec_ref, sgt_ref, base_ref, *refs):
    first = stages[0][1]
    out_refs = refs[:first]
    rec_s, x_s, p_s, slip_s, sgt_s, base_s, tab_s, sems = refs[first:]
    devices, capacity, width = rec_ref.shape
    slots = devices * capacity
    n_time = sgt_ref.shape[2]
    half = n_time // 2
    wide = n_time // 4
    block_wide = n_time // 8
    n_slip = width - 128
    base_copy = pltpu.make_async_copy(base_ref, base_s, sems.at[3])
    base_copy.start()
    copies = []
    for c in range(3):
        at = slice(6 * c, 6 * c + 6)
        copies.append(pltpu.make_async_copy(sgt_ref.at[at], sgt_s.at[at], sems.at[c]))
        copies[c].start()
    for d in range(devices):
        rec_s[d * capacity : (d + 1) * capacity, :] = rec_ref[d].astype(F32)
    tail = rec_s[:, n_slip:]
    row = tail[:, ROW_LANE : ROW_LANE + 1]
    here = iota((slots, PTS), 1).astype(F32) == row
    left = jnp.concatenate(
        [
            jnp.concatenate(
                [jnp.where(here, tail[:, 6 * p + m : 6 * p + m + 1], 0.0).astype(BF16) for m in range(6)],
                axis=1,
            )
            for p in range(2)
        ],
        axis=0,
    )
    base_copy.wait()
    for block in range(4):
        forward_table(base_s, tab_s, block)
    slip = rec_s[:, :n_slip].astype(BF16)
    for block in range(4):
        cols = slice(2 * block * block_wide, 2 * (block + 1) * block_wide)
        slip_s[:, cols] = nn(slip, tab_s[:, cols])
    ruptures = math.prod(radix for _, radix, _, _ in stages)
    shape = (ruptures, slots)
    rup = nt((iota((8, 128), 1) == RUP_LANE).astype(F32).astype(BF16), tail.astype(BF16))[:1].astype(jnp.int32)
    worker = (iota((1, slots), 1) // capacity) % lax.axis_size("worker")
    apart = {"worker": worker ^ lax.axis_index("worker"), "server": rup ^ lax.axis_index("server")}
    where_to = ordered(stages, apart)
    seg = (iota(shape, 0) == where_to).astype(F32).astype(BF16)
    seg = jnp.concatenate([seg, seg], axis=1)
    part = ruptures // first
    for c in range(3):
        copies[c].wait()
        x = []
        for k in range(4):
            rows = sgt_s[6 * c : 6 * c + 6, :, k * wide : (k + 1) * wide].reshape(6 * PTS, wide)
            out = nn(left, rows)
            x.append(out[:slots] + out[slots:])
        plus = (x[0] + x[2], x[1] + x[3])
        x_s[c, :slots, :] = (plus[0] + plus[1]).astype(BF16)
        x_s[c, slots : 2 * slots, :] = (plus[0] - plus[1]).astype(BF16)
        x_s[c, 2 * slots : 3 * slots, :] = (x[0] - x[2]).astype(BF16)
        x_s[c, 3 * slots :, :] = (x[1] - x[3]).astype(BF16)
        for block in range(4):
            first_row, last_row = ((0, 1), (1, 2), (2, 4), (2, 4))[block]
            middle = (2 * block + 1) * block_wide
            cols = slice(middle - block_wide, middle)
            cols_im = slice(middle, middle + block_wide)
            product = nn(
                x_s[c, first_row * slots : last_row * slots, :],
                tab_s[:, middle - block_wide : middle + block_wide],
            )
            t_re = product[:slots, :block_wide]
            t_im = product[:slots, block_wide:]
            if block == 2:
                t_re, t_im = t_re + product[slots:, block_wide:], t_im - product[slots:, :block_wide]
            elif block == 3:
                t_re, t_im = t_re - product[slots:, block_wide:], t_im + product[slots:, :block_wide]
            slip_re = slip_s[:, cols]
            slip_im = slip_s[:, cols_im]
            hi, lo = hilo(slip_re * t_re - slip_im * t_im)
            p_s[:slots, cols] = hi
            p_s[slots:, cols] = lo
            hi, lo = hilo(slip_re * t_im + slip_im * t_re)
            p_s[:slots, cols_im] = hi
            p_s[slots:, cols_im] = lo
        total = nn(seg, p_s[...])
        for block in range(4):
            for k in range(first):
                ref = out_refs[k]
                for p in range(2):
                    at = slice(p * half + block * block_wide, p * half + (block + 1) * block_wide)
                    ref[c, :, at] = total[
                        k * part : (k + 1) * part, (2 * block + p) * block_wide : (2 * block + p + 1) * block_wide
                    ].astype(ref.dtype)


def sum_kernel(radix, *refs):
    own_ref = refs[0]
    out_refs = refs[-radix:]
    part = out_refs[0].shape[1]
    for c in range(3):
        total = own_ref[c]
        for ref in refs[1:-radix]:
            total = total + ref[c].astype(F32)
        for k in range(radix):
            out_refs[k][c] = total[k * part : (k + 1) * part].astype(out_refs[k].dtype)


def inverse_table_kernel(base_ref, hi_ref, lo_ref):
    block_wide = hi_ref.shape[0] // 4
    count = block_wide // STEP
    wide = 256
    for p in range(2):
        fine = 2 * count + 2 * p * STEP
        for lc in range(hi_ref.shape[1] // wide):
            sl = slice(lc * wide, (lc + 1) * wide)
            cf = base_ref[fine : fine + STEP, sl]
            sf = base_ref[fine + STEP : fine + 2 * STEP, sl]

            def table(a, carry):
                ca = base_ref[pl.ds(a, 1), sl]
                sa = base_ref[pl.ds(count + a, 1), sl]
                for base, value in ((0, ca * cf - sa * sf), (block_wide, -(sa * cf + ca * sf))):
                    at = pl.ds(pl.multiple_of(2 * p * block_wide + base + a * STEP, STEP), STEP)
                    hi, lo = hilo(value)
                    hi_ref[at, sl] = hi
                    lo_ref[at, sl] = lo
                return carry

            lax.fori_loop(0, count, table, 0)


def gain_kernel(gr_ref, gi_ref):
    half = gr_ref.shape[1]
    block_wide = half // 4
    n_time = 2 * half
    shape = gr_ref.shape
    low = math.log(4.0 / n_time)
    high = math.log(0.25)
    period = iota(shape, 0)
    slot = iota(shape, 1)
    block = slot // block_wide
    freq = 4 * (slot % block_wide) + jnp.where(block < 2, 2 * block, 2 * block - 3)
    omega_freq = freq.astype(F32) * (2.0 * math.pi / n_time)
    omega_osc = 2.0 * math.pi * jnp.exp(low + (high - low) * period.astype(F32) / (PERIODS - 1))
    den_real = omega_osc * omega_osc - omega_freq * omega_freq
    den_imag = 2.0 * DAMPING * omega_osc * omega_freq
    weight = jnp.where(freq == 0, 1.0, 2.0) / n_time
    gain = weight * (omega_osc * omega_osc / (den_real * den_real + den_imag * den_imag))
    gr_ref[...] = jnp.where(period < PERIODS, -gain * den_real, weight)
    gi_ref[...] = jnp.where(period < PERIODS, -gain * den_imag, 0.0)


def final_kernel(count, *refs):
    spec_refs = refs[:count]
    *tables, gr_ref, gi_ref, seis_ref, peak_ref = refs[count:]
    half = gr_ref.shape[1]
    block_wide = half // 4
    wide = half // 2
    spec = []
    for c in range(3):
        total = spec_refs[0][c]
        for ref in spec_refs[1:]:
            total = total + ref[c].astype(F32)
        spec.append(total)
    gr = gr_ref[...]
    gi = gi_ref[...]

    def accel(block):
        cols = slice(block * block_wide, (block + 1) * block_wide)
        cols_im = slice(half + block * block_wide, half + (block + 1) * block_wide)
        g_re = gr[:, cols]
        g_im = gi[:, cols]
        re = jnp.concatenate([s[:, cols] * g_re + s[:, cols_im] * g_im for s in spec], axis=0)
        im = jnp.concatenate([s[:, cols_im] * g_re - s[:, cols] * g_im for s in spec], axis=0)
        return re, im

    def product(left, hi_tab, lo_tab):
        count = left.shape[0]
        hi, lo = hilo(left)
        both = nn(jnp.concatenate([hi, lo], axis=0), hi_tab)
        return both[:count] + both[count:] + nn(hi, lo_tab)

    even_hi, even_lo, odd_hi, odd_lo = tables
    pair = [
        product(
            jnp.concatenate(accel(block), axis=1),
            even_hi[block * wide : (block + 1) * wide, :],
            even_lo[block * wide : (block + 1) * wide, :],
        )
        for block in range(2)
    ]
    re_c, im_c = accel(2)
    re_d, im_d = accel(3)
    straight = jnp.concatenate([re_c, im_c, re_d, im_d], axis=1)
    turned = jnp.concatenate([-im_c, re_c, im_d, -re_d], axis=1)
    odd = product(jnp.concatenate([straight, turned], axis=0), odd_hi[...], odd_lo[...])
    evens = (pair[0] + pair[1], pair[0] - pair[1])
    odds = (odd[: 3 * ROWS], odd[3 * ROWS :])
    peak = jnp.max(
        jnp.maximum(jnp.abs(evens[0]) + jnp.abs(odds[0]), jnp.abs(evens[1]) + jnp.abs(odds[1])),
        axis=1,
        keepdims=True,
    )
    for c in range(3):
        row = c * ROWS + PERIODS
        for k in range(2):
            e = evens[k][row : row + 1]
            o = odds[k][row : row + 1]
            seis_ref[c, :, k * wide : (k + 1) * wide] = e + o
            seis_ref[c, :, half + k * wide : half + (k + 1) * wide] = e - o
        column = jnp.broadcast_to(peak[c * ROWS : (c + 1) * ROWS], (ROWS, 128))
        column = jnp.concatenate([column, jnp.zeros((128 - ROWS, 128), F32)], axis=0)
        peak_ref[c] = column.T[:1, :PERIODS]


def vmem():
    return pl.BlockSpec(memory_space=pltpu.VMEM)


def hbm():
    return pl.BlockSpec(memory_space=pltpu.HBM)


def in_hbm(x):
    return pltpu.with_memory_space_constraint(x, pltpu.HBM)


def params(mib):
    return pltpu.CompilerParams(vmem_limit_bytes=mib << 20)


def exchange_plan(n_worker, n_server):
    stages = []
    for axis, size in (("worker", n_worker), ("server", n_server)):
        bits = size.bit_length() - 1
        assert size == 1 << bits
        shift = 0
        while shift < bits:
            step = 1 if (bits - shift) % 2 else 2
            stages.append((axis, 1 << step, shift, size))
            shift += step
    return stages


def send(parts, stage):
    axis, radix, shift, size = stage
    return [
        lax.ppermute(parts[k], axis, [(i, i ^ (k << shift)) for i in range(size)])
        for k in range(radix - 1, 0, -1)
    ]


def beside(kernel, base, own):
    base, own = lax.optimization_barrier((jnp.asarray(base), own))
    own, *made = lax.optimization_barrier((own, *kernel(base)))
    return own, made


def sent_type(stages, i):
    return F32 if i == 0 or i == len(stages) - 1 else BF16


def shards(n_server, n_worker, sgt, ownership, sub_points, moments, slip):
    devices = n_server * n_worker
    n_time = sgt.shape[2]
    half = n_time // 2
    rup_w = sub_points.shape[1]
    sub_dev = sub_points.shape[2]
    n_slip = slip.shape[3]
    capacity = 4 * sub_dev // (3 * n_worker)
    slots = devices * capacity
    width = n_slip + 128
    stages = exchange_plan(n_worker, n_server)
    assert rup_w == n_server and sgt.shape[0] == PTS and slots % 16 == 0 and 4 * n_slip == n_time

    record = pl.pallas_call(
        pack_kernel,
        out_shape=jax.ShapeDtypeStruct((devices, capacity, width), BF16),
        in_specs=[hbm()] * 4,
        out_specs=vmem(),
        scratch_shapes=[
            pltpu.VMEM((slots, width), F32),
            pltpu.VMEM((ownership.shape[0] // 128, 128), jnp.int32),
            pltpu.VMEM((rup_w, sub_dev), jnp.int32),
            pltpu.VMEM((6, rup_w, sub_dev), F32),
            pltpu.VMEM((rup_w, sub_dev, n_slip), BF16),
            pltpu.SemaphoreType.DMA((4,)),
        ],
        compiler_params=params(12),
        name="pack",
    )(
        *[
            in_hbm(x)
            for x in (
                ownership.reshape(-1, 128),
                sub_points[0],
                jnp.transpose(moments[0], (1, 0, 2)),
                slip[0],
            )
        ]
    )
    record = lax.all_to_all(record, ("server", "worker"), split_axis=0, concat_axis=0, tiled=True)
    base = jnp.asarray(forward_base(n_time))

    inverse = pl.pallas_call(
        inverse_table_kernel,
        out_shape=[jax.ShapeDtypeStruct((half, half // 2), BF16)] * 2,
        in_specs=[vmem()],
        out_specs=[vmem()] * 2,
        compiler_params=params(8),
        cost_estimate=pl.CostEstimate(flops=10**9, bytes_accessed=10**7, transcendentals=0),
        name="inverse_table",
    )
    gain = pl.pallas_call(
        gain_kernel,
        out_shape=[jax.ShapeDtypeStruct((ROWS, half), F32)] * 2,
        out_specs=[vmem()] * 2,
        compiler_params=params(2),
        name="gain",
    )()
    tables = []
    bases = inverse_bases(n_time)

    def part_shapes(i):
        count = math.prod(radix for _, radix, _, _ in stages[i + 1 :])
        return [
            jax.ShapeDtypeStruct((3, count, n_time), sent_type(stages, i) if k else F32)
            for k in range(stages[i][1])
        ]

    parts = pl.pallas_call(
        functools.partial(owner_kernel, stages),
        out_shape=part_shapes(0),
        in_specs=[vmem()] + [hbm()] * 2,
        out_specs=[vmem()] * stages[0][1],
        scratch_shapes=[
            pltpu.VMEM((slots, width), F32),
            pltpu.VMEM((3, 4 * slots, n_slip), BF16),
            pltpu.VMEM((2 * slots, n_time), BF16),
            pltpu.VMEM((slots, n_time), F32),
            pltpu.VMEM((18, PTS, n_time), BF16),
            pltpu.VMEM(base.shape, F32),
            pltpu.VMEM((half // 2, n_time), BF16),
            pltpu.SemaphoreType.DMA((4,)),
        ],
        compiler_params=params(36),
        cost_estimate=pl.CostEstimate(flops=10**10, bytes_accessed=2 * 10**7, transcendentals=0),
        name="owner",
    )(record, in_hbm(jnp.transpose(sgt, (1, 0, 2))), in_hbm(base))
    arrived = send(parts, stages[0])
    for i in range(1, len(stages)):
        radix = stages[i][1]
        parts = pl.pallas_call(
            functools.partial(sum_kernel, radix),
            out_shape=part_shapes(i),
            in_specs=[vmem()] * (1 + len(arrived)),
            out_specs=[vmem()] * radix,
            compiler_params=params(4),
            name=f"sum_{i}",
        )(parts[0], *arrived)
        arrived = send(parts, stages[i])
        if i >= len(stages) - 2:
            own, pair = beside(inverse, bases[len(tables) // 2], parts[0])
            parts = [own]
            tables += pair
    count = 1 + len(arrived)
    seis, peaks = pl.pallas_call(
        functools.partial(final_kernel, count),
        out_shape=[
            jax.ShapeDtypeStruct((3, 1, n_time), F32),
            jax.ShapeDtypeStruct((3, 1, PERIODS), F32),
        ],
        in_specs=[vmem()] * (count + 6),
        out_specs=[vmem()] * 2,
        compiler_params=params(20),
        name="finish",
    )(parts[0], *arrived, *tables, *gain)
    return (
        jnp.transpose(seis, (1, 0, 2)).reshape(1, 1, 3, n_time),
        jnp.transpose(peaks, (1, 0, 2)).reshape(1, 1, 3, PERIODS),
    )


def solution(mesh):
    placed = (
        P(("server", "worker"), None, None),
        P(),
        P("worker", None, "server"),
        P("worker", None, None, "server"),
        P("worker", None, "server", None),
    )
    return jax.shard_map(
        functools.partial(shards, mesh.shape["server"], mesh.shape["worker"]),
        mesh=mesh,
        in_specs=placed,
        out_specs=(P("worker", "server", None, None), P("worker", "server", None, None)),
        check_vma=False,
    )
```

```python
import functools
import math

import jax
import jax.numpy as jnp
import numpy as np
from jax import lax
from jax.experimental import pallas as pl
from jax.experimental.pallas import tpu as pltpu
from jax.sharding import PartitionSpec as P

PERIODS = 44
DAMPING = 0.05
ROWS = 48
STEP = 32
PTS = 128
EARLY = 3
RESIDUES = (0, 2, 1, 3)
ROW_LANE = 64
RUP_LANE = 96
F32 = jnp.float32
BF16 = jnp.bfloat16


def nn(a, b):
    return lax.dot_general(a, b, (((1,), (0,)), ((), ())), preferred_element_type=F32)


def nt(a, b):
    return lax.dot_general(a, b, (((1,), (1,)), ((), ())), preferred_element_type=F32)


def iota(shape, dim):
    return lax.broadcasted_iota(jnp.int32, shape, dim)


def hilo(x):
    hi = x.astype(BF16)
    return hi, (x - hi.astype(F32)).astype(BF16)


def angle(product, n_time):
    return (2.0 * math.pi / n_time) * (product % n_time)


def cos_sin(*angles):
    return np.concatenate([f(x) for x in angles for f in (np.cos, np.sin)]).astype(np.float32)


def forward_base(n_time):
    index = np.arange(n_time // 8)
    freq = np.concatenate([4 * index + residue for residue in RESIDUES])
    coarse = angle(np.arange(n_time // 4 // STEP)[:, None] * STEP * freq[None, :], n_time)
    fine = angle(np.arange(STEP)[:, None] * freq[None, :], n_time)
    return cos_sin(coarse, fine)


def inverse_bases(n_time):
    time = np.arange(n_time // 4)
    coarse = angle(np.arange(n_time // 8 // STEP)[:, None] * 4 * STEP * time[None, :], n_time)
    fine = [
        angle((np.arange(STEP)[:, None] * 4 + residue) * time[None, :], n_time)
        for residue in RESIDUES
    ]
    return [cos_sin(coarse, *fine[:2]), cos_sin(coarse, *fine[2:])]


def ordered(stages, apart):
    place = jnp.zeros_like(apart["worker"])
    for axis, radix, shift, _ in stages:
        place = place * radix + ((apart[axis] >> shift) & (radix - 1))
    return place


def pack_kernel(*refs):
    sources = (*refs[:5], refs[5].at[:EARLY])
    out_ref, kept_ref, rows_ref, scr, own_ref, pts_ref, mom_ref, slip_ref, sems = refs[6:]
    copies = [
        pltpu.make_async_copy(src, dst, sems.at[i])
        for i, (src, dst) in enumerate(zip(sources, (own_ref, pts_ref, mom_ref, slip_ref, kept_ref, rows_ref)))
    ]
    for copy in copies:
        copy.start()
    devices, capacity, _ = out_ref.shape
    slots = devices * capacity
    rup_w, sub = pts_ref.shape
    asked = rup_w * sub
    n_slip = slip_ref.shape[2]
    earlier = (iota((asked, asked), 0) < iota((asked, asked), 1)).astype(F32).astype(BF16)
    spread = iota((128, 6), 0)
    comp = iota((128, 6), 1)
    spread_hi = (spread == comp).astype(F32).astype(BF16)
    spread_lo = (spread == comp + 6).astype(F32).astype(BF16)
    for copy in copies[:4]:
        copy.wait()
    own = own_ref[...]
    blocks = own.shape[0]
    both = jnp.concatenate([own // PTS, own % PTS], axis=0).astype(F32).astype(BF16)
    p = jnp.concatenate([pts_ref[r : r + 1, :] for r in range(rup_w)], axis=1)
    in_lane = (iota((128, asked), 0) == p % 128).astype(F32).astype(BF16)
    found = nn(both, in_lane)
    in_block = (iota((blocks, asked), 0) == p // 128).astype(F32)
    dev = jnp.sum(found[:blocks] * in_block, axis=0, keepdims=True)
    loc = jnp.sum(found[blocks:] * in_block, axis=0, keepdims=True)
    onehot = (iota((devices, asked), 0).astype(F32) == dev).astype(F32)
    before = nn(onehot.astype(BF16), earlier)
    rank = jnp.sum(before * onehot, axis=0, keepdims=True)
    target = dev * capacity + rank
    pick = (iota((slots, asked), 0).astype(F32) == target).astype(F32)
    pick16 = pick.astype(BF16)
    mom = jnp.concatenate(
        [
            jnp.concatenate([mom_ref[m, r : r + 1, :] for r in range(rup_w)], axis=1)
            for m in range(6)
        ],
        axis=0,
    )
    hi, lo = hilo(mom)
    rup = (iota((1, asked), 1) // sub).astype(F32)
    lane = iota((128, asked), 0)
    expanded = nn(spread_hi, hi) + nn(spread_lo, lo)
    expanded = jnp.where(lane == ROW_LANE, loc, jnp.where(lane == RUP_LANE, rup, expanded))
    scr[:, n_slip:] = nt(pick16, expanded.astype(BF16))
    slip = slip_ref[...].astype(F32).reshape(asked, n_slip).astype(BF16)
    scr[:, :n_slip] = nn(pick16, slip)
    for d in range(devices):
        out_ref[d] = scr[d * capacity : (d + 1) * capacity, :].astype(BF16)
    for copy in copies[4:]:
        copy.wait()


def forward_table(base_ref, tab_ref, block):
    count = tab_ref.shape[0] // STEP
    wide = tab_ref.shape[1] // 8
    sl = slice(block * wide, (block + 1) * wide)
    cols = slice(2 * block * wide, (2 * block + 1) * wide)
    cols_im = slice((2 * block + 1) * wide, (2 * block + 2) * wide)
    cb = base_ref[2 * count : 2 * count + STEP, sl]
    sb = base_ref[2 * count + STEP :, sl]

    def table(a, carry):
        ca = base_ref[pl.ds(a, 1), sl]
        sa = base_ref[pl.ds(count + a, 1), sl]
        at = pl.ds(pl.multiple_of(a * STEP, STEP), STEP)
        tab_ref[at, cols] = (ca * cb - sa * sb).astype(BF16)
        tab_ref[at, cols_im] = (-(sa * cb + ca * sb)).astype(BF16)
        return carry

    lax.fori_loop(0, count, table, 0, unroll=4)


def owner_kernel(stages, rec_ref, sgt_ref, base_ref, rows_ref, *refs):
    first = stages[0][1]
    out_refs = refs[:first]
    rec_s, x_s, p_s, slip_s, sgt_s, tab_s, sems = refs[first:]
    devices, capacity, width = rec_ref.shape
    slots = devices * capacity
    n_time = sgt_ref.shape[2]
    half = n_time // 2
    wide = n_time // 4
    block_wide = n_time // 8
    n_slip = width - 128
    copies = []
    for c in range(3):
        at = slice(6 * c if c else EARLY, 6 * c + 6)
        copies.append(pltpu.make_async_copy(sgt_ref.at[at], sgt_s.at[at], sems.at[c]))
        copies[c].start()
    for d in range(devices):
        rec_s[d * capacity : (d + 1) * capacity, :] = rec_ref[d].astype(F32)
    tail = rec_s[:, n_slip:]
    row = tail[:, ROW_LANE : ROW_LANE + 1]
    here = iota((slots, PTS), 1).astype(F32) == row
    left = jnp.concatenate(
        [
            jnp.concatenate(
                [jnp.where(here, tail[:, 6 * p + m : 6 * p + m + 1], 0.0).astype(BF16) for m in range(6)],
                axis=1,
            )
            for p in range(2)
        ],
        axis=0,
    )
    for block in range(4):
        forward_table(base_ref, tab_s, block)
    slip = rec_s[:, :n_slip].astype(BF16)
    for block in range(4):
        cols = slice(2 * block * block_wide, 2 * (block + 1) * block_wide)
        slip_s[:, cols] = nn(slip, tab_s[:, cols])
    ruptures = math.prod(radix for _, radix, _, _ in stages)
    shape = (ruptures, slots)
    rup = nt((iota((8, 128), 1) == RUP_LANE).astype(F32).astype(BF16), tail.astype(BF16))[:1].astype(jnp.int32)
    worker = (iota((1, slots), 1) // capacity) % lax.axis_size("worker")
    apart = {"worker": worker ^ lax.axis_index("worker"), "server": rup ^ lax.axis_index("server")}
    where_to = ordered(stages, apart)
    seg = (iota(shape, 0) == where_to).astype(F32).astype(BF16)
    seg = jnp.concatenate([seg, seg], axis=1)
    part = ruptures // first
    for c in range(3):
        copies[c].wait()
        x = []
        for k in range(4):
            cols = slice(k * wide, (k + 1) * wide)
            rows = sgt_s[6 * c if c else EARLY : 6 * c + 6, :, cols].reshape(-1, wide)
            if c == 0:
                rows = jnp.concatenate([rows_ref[:, :, cols].reshape(-1, wide), rows], axis=0)
            out = nn(left, rows)
            x.append(out[:slots] + out[slots:])
        plus = (x[0] + x[2], x[1] + x[3])
        x_s[c, :slots, :] = (plus[0] + plus[1]).astype(BF16)
        x_s[c, slots : 2 * slots, :] = (plus[0] - plus[1]).astype(BF16)
        x_s[c, 2 * slots : 3 * slots, :] = (x[0] - x[2]).astype(BF16)
        x_s[c, 3 * slots :, :] = (x[1] - x[3]).astype(BF16)
        for block in range(4):
            first_row, last_row = ((0, 1), (1, 2), (2, 4), (2, 4))[block]
            middle = (2 * block + 1) * block_wide
            cols = slice(middle - block_wide, middle)
            cols_im = slice(middle, middle + block_wide)
            product = nn(
                x_s[c, first_row * slots : last_row * slots, :],
                tab_s[:, middle - block_wide : middle + block_wide],
            )
            t_re = product[:slots, :block_wide]
            t_im = product[:slots, block_wide:]
            if block == 2:
                t_re, t_im = t_re + product[slots:, block_wide:], t_im - product[slots:, :block_wide]
            elif block == 3:
                t_re, t_im = t_re - product[slots:, block_wide:], t_im + product[slots:, :block_wide]
            slip_re = slip_s[:, cols]
            slip_im = slip_s[:, cols_im]
            hi, lo = hilo(slip_re * t_re - slip_im * t_im)
            p_s[:slots, cols] = hi
            p_s[slots:, cols] = lo
            hi, lo = hilo(slip_re * t_im + slip_im * t_re)
            p_s[:slots, cols_im] = hi
            p_s[slots:, cols_im] = lo
        total = nn(seg, p_s[...])
        for block in range(4):
            for k in range(first):
                ref = out_refs[k]
                for p in range(2):
                    at = slice(p * half + block * block_wide, p * half + (block + 1) * block_wide)
                    ref[c, :, at] = total[
                        k * part : (k + 1) * part, (2 * block + p) * block_wide : (2 * block + p + 1) * block_wide
                    ].astype(ref.dtype)


def sum_kernel(radix, *refs):
    own_ref = refs[0]
    out_refs = refs[-radix:]
    part = out_refs[0].shape[1]
    for c in range(3):
        total = own_ref[c]
        for ref in refs[1:-radix]:
            total = total + ref[c].astype(F32)
        for k in range(radix):
            out_refs[k][c] = total[k * part : (k + 1) * part].astype(out_refs[k].dtype)


def inverse_table_kernel(base_ref, hi_ref, lo_ref):
    block_wide = hi_ref.shape[0] // 4
    count = block_wide // STEP
    wide = 256
    for p in range(2):
        fine = 2 * count + 2 * p * STEP
        for lc in range(hi_ref.shape[1] // wide):
            sl = slice(lc * wide, (lc + 1) * wide)
            cf = base_ref[fine : fine + STEP, sl]
            sf = base_ref[fine + STEP : fine + 2 * STEP, sl]

            def table(a, carry):
                ca = base_ref[pl.ds(a, 1), sl]
                sa = base_ref[pl.ds(count + a, 1), sl]
                for base, value in ((0, ca * cf - sa * sf), (block_wide, -(sa * cf + ca * sf))):
                    at = pl.ds(pl.multiple_of(2 * p * block_wide + base + a * STEP, STEP), STEP)
                    hi, lo = hilo(value)
                    hi_ref[at, sl] = hi
                    lo_ref[at, sl] = lo
                return carry

            lax.fori_loop(0, count, table, 0)


def gain_kernel(gr_ref, gi_ref):
    half = gr_ref.shape[1]
    block_wide = half // 4
    n_time = 2 * half
    shape = gr_ref.shape
    low = math.log(4.0 / n_time)
    high = math.log(0.25)
    period = iota(shape, 0)
    slot = iota(shape, 1)
    block = slot // block_wide
    freq = 4 * (slot % block_wide) + jnp.where(block < 2, 2 * block, 2 * block - 3)
    omega_freq = freq.astype(F32) * (2.0 * math.pi / n_time)
    omega_osc = 2.0 * math.pi * jnp.exp(low + (high - low) * period.astype(F32) / (PERIODS - 1))
    den_real = omega_osc * omega_osc - omega_freq * omega_freq
    den_imag = 2.0 * DAMPING * omega_osc * omega_freq
    weight = jnp.where(freq == 0, 1.0, 2.0) / n_time
    gain = weight * (omega_osc * omega_osc / (den_real * den_real + den_imag * den_imag))
    gr_ref[...] = jnp.where(period < PERIODS, -gain * den_real, weight)
    gi_ref[...] = jnp.where(period < PERIODS, -gain * den_imag, 0.0)


def final_kernel(count, *refs):
    spec_refs = refs[:count]
    *tables, gr_ref, gi_ref, seis_ref, peak_ref = refs[count:]
    half = gr_ref.shape[1]
    block_wide = half // 4
    wide = half // 2
    spec = []
    for c in range(3):
        total = spec_refs[0][c]
        for ref in spec_refs[1:]:
            total = total + ref[c].astype(F32)
        spec.append(total)
    gr = gr_ref[...]
    gi = gi_ref[...]

    def accel(block):
        cols = slice(block * block_wide, (block + 1) * block_wide)
        cols_im = slice(half + block * block_wide, half + (block + 1) * block_wide)
        g_re = gr[:, cols]
        g_im = gi[:, cols]
        re = jnp.concatenate([s[:, cols] * g_re + s[:, cols_im] * g_im for s in spec], axis=0)
        im = jnp.concatenate([s[:, cols_im] * g_re - s[:, cols] * g_im for s in spec], axis=0)
        return re, im

    def product(left, hi_tab, lo_tab):
        count = left.shape[0]
        hi, lo = hilo(left)
        both = nn(jnp.concatenate([hi, lo], axis=0), hi_tab)
        return both[:count] + both[count:] + nn(hi, lo_tab)

    even_hi, even_lo, odd_hi, odd_lo = tables
    pair = [
        product(
            jnp.concatenate(accel(block), axis=1),
            even_hi[block * wide : (block + 1) * wide, :],
            even_lo[block * wide : (block + 1) * wide, :],
        )
        for block in range(2)
    ]
    re_c, im_c = accel(2)
    re_d, im_d = accel(3)
    straight = jnp.concatenate([re_c, im_c, re_d, im_d], axis=1)
    turned = jnp.concatenate([-im_c, re_c, im_d, -re_d], axis=1)
    odd = product(jnp.concatenate([straight, turned], axis=0), odd_hi[...], odd_lo[...])
    evens = (pair[0] + pair[1], pair[0] - pair[1])
    odds = (odd[: 3 * ROWS], odd[3 * ROWS :])
    peak = jnp.max(
        jnp.maximum(jnp.abs(evens[0]) + jnp.abs(odds[0]), jnp.abs(evens[1]) + jnp.abs(odds[1])),
        axis=1,
        keepdims=True,
    )
    for c in range(3):
        row = c * ROWS + PERIODS
        for k in range(2):
            e = evens[k][row : row + 1]
            o = odds[k][row : row + 1]
            seis_ref[c, :, k * wide : (k + 1) * wide] = e + o
            seis_ref[c, :, half + k * wide : half + (k + 1) * wide] = e - o
        column = jnp.broadcast_to(peak[c * ROWS : (c + 1) * ROWS], (ROWS, 128))
        column = jnp.concatenate([column, jnp.zeros((128 - ROWS, 128), F32)], axis=0)
        peak_ref[c] = column.T[:1, :PERIODS]


def vmem():
    return pl.BlockSpec(memory_space=pltpu.VMEM)


def hbm():
    return pl.BlockSpec(memory_space=pltpu.HBM)


def in_hbm(x):
    return pltpu.with_memory_space_constraint(x, pltpu.HBM)


def params(mib):
    return pltpu.CompilerParams(vmem_limit_bytes=mib << 20)


def exchange_plan(n_worker, n_server):
    stages = []
    for axis, size in (("worker", n_worker), ("server", n_server)):
        bits = size.bit_length() - 1
        assert size == 1 << bits
        shift = 0
        while shift < bits:
            step = 1 if (bits - shift) % 2 else 2
            stages.append((axis, 1 << step, shift, size))
            shift += step
    return stages


def send(parts, stage):
    axis, radix, shift, size = stage
    return [
        lax.ppermute(parts[k], axis, [(i, i ^ (k << shift)) for i in range(size)])
        for k in range(radix - 1, 0, -1)
    ]


def beside(kernel, base, own):
    base, own = lax.optimization_barrier((jnp.asarray(base), own))
    own, *made = lax.optimization_barrier((own, *kernel(base)))
    return own, made


def sent_type(stages, i):
    return F32 if i == 0 or i == len(stages) - 1 else BF16


def shards(n_server, n_worker, sgt, ownership, sub_points, moments, slip):
    devices = n_server * n_worker
    n_time = sgt.shape[2]
    half = n_time // 2
    rup_w = sub_points.shape[1]
    sub_dev = sub_points.shape[2]
    n_slip = slip.shape[3]
    capacity = 4 * sub_dev // (3 * n_worker)
    slots = devices * capacity
    width = n_slip + 128
    stages = exchange_plan(n_worker, n_server)
    assert rup_w == n_server and sgt.shape[0] == PTS and slots % 16 == 0 and 4 * n_slip == n_time

    base = jnp.asarray(forward_base(n_time))
    sgt = in_hbm(jnp.transpose(sgt, (1, 0, 2)))
    record, base, rows = pl.pallas_call(
        pack_kernel,
        out_shape=[
            jax.ShapeDtypeStruct((devices, capacity, width), BF16),
            jax.ShapeDtypeStruct(base.shape, F32),
            jax.ShapeDtypeStruct((EARLY, PTS, n_time), BF16),
        ],
        in_specs=[hbm()] * 6,
        out_specs=[vmem()] * 3,
        scratch_shapes=[
            pltpu.VMEM((slots, width), F32),
            pltpu.VMEM((ownership.shape[0] // 128, 128), jnp.int32),
            pltpu.VMEM((rup_w, sub_dev), jnp.int32),
            pltpu.VMEM((6, rup_w, sub_dev), F32),
            pltpu.VMEM((rup_w, sub_dev, n_slip), BF16),
            pltpu.SemaphoreType.DMA((6,)),
        ],
        compiler_params=params(16),
        name="pack",
    )(
        *[
            in_hbm(x)
            for x in (
                ownership.reshape(-1, 128),
                sub_points[0],
                jnp.transpose(moments[0], (1, 0, 2)),
                slip[0],
                base,
                sgt,
            )
        ]
    )
    record = lax.all_to_all(record, ("server", "worker"), split_axis=0, concat_axis=0, tiled=True)

    inverse = pl.pallas_call(
        inverse_table_kernel,
        out_shape=[jax.ShapeDtypeStruct((half, half // 2), BF16)] * 2,
        in_specs=[vmem()],
        out_specs=[vmem()] * 2,
        compiler_params=params(8),
        cost_estimate=pl.CostEstimate(flops=10**9, bytes_accessed=10**7, transcendentals=0),
        name="inverse_table",
    )
    gain = pl.pallas_call(
        gain_kernel,
        out_shape=[jax.ShapeDtypeStruct((ROWS, half), F32)] * 2,
        out_specs=[vmem()] * 2,
        compiler_params=params(2),
        name="gain",
    )()
    tables = []
    bases = inverse_bases(n_time)

    def part_shapes(i):
        count = math.prod(radix for _, radix, _, _ in stages[i + 1 :])
        return [
            jax.ShapeDtypeStruct((3, count, n_time), sent_type(stages, i) if k else F32)
            for k in range(stages[i][1])
        ]

    parts = pl.pallas_call(
        functools.partial(owner_kernel, stages),
        out_shape=part_shapes(0),
        in_specs=[vmem(), hbm(), vmem(), vmem()],
        out_specs=[vmem()] * stages[0][1],
        scratch_shapes=[
            pltpu.VMEM((slots, width), F32),
            pltpu.VMEM((3, 4 * slots, n_slip), BF16),
            pltpu.VMEM((2 * slots, n_time), BF16),
            pltpu.VMEM((slots, n_time), F32),
            pltpu.VMEM((18, PTS, n_time), BF16),
            pltpu.VMEM((half // 2, n_time), BF16),
            pltpu.SemaphoreType.DMA((4,)),
        ],
        compiler_params=params(36),
        cost_estimate=pl.CostEstimate(flops=10**10, bytes_accessed=2 * 10**7, transcendentals=0),
        name="owner",
    )(record, sgt, base, rows)
    arrived = send(parts, stages[0])
    for i in range(1, len(stages)):
        radix = stages[i][1]
        parts = pl.pallas_call(
            functools.partial(sum_kernel, radix),
            out_shape=part_shapes(i),
            in_specs=[vmem()] * (1 + len(arrived)),
            out_specs=[vmem()] * radix,
            compiler_params=params(4),
            name=f"sum_{i}",
        )(parts[0], *arrived)
        arrived = send(parts, stages[i])
        if i >= len(stages) - 2:
            own, pair = beside(inverse, bases[len(tables) // 2], parts[0])
            parts = [own]
            tables += pair
    count = 1 + len(arrived)
    seis, peaks = pl.pallas_call(
        functools.partial(final_kernel, count),
        out_shape=[
            jax.ShapeDtypeStruct((3, 1, n_time), F32),
            jax.ShapeDtypeStruct((3, 1, PERIODS), F32),
        ],
        in_specs=[vmem()] * (count + 6),
        out_specs=[vmem()] * 2,
        compiler_params=params(20),
        name="finish",
    )(parts[0], *arrived, *tables, *gain)
    return (
        jnp.transpose(seis, (1, 0, 2)).reshape(1, 1, 3, n_time),
        jnp.transpose(peaks, (1, 0, 2)).reshape(1, 1, 3, PERIODS),
    )


def solution(mesh):
    placed = (
        P(("server", "worker"), None, None),
        P(),
        P("worker", None, "server"),
        P("worker", None, None, "server"),
        P("worker", None, "server", None),
    )
    return jax.shard_map(
        functools.partial(shards, mesh.shape["server"], mesh.shape["worker"]),
        mesh=mesh,
        in_specs=placed,
        out_specs=(P("worker", "server", None, None), P("worker", "server", None, None)),
        check_vma=False,
    )
```

```python
import functools
import math

import jax
import jax.numpy as jnp
import numpy as np
from jax import lax
from jax.experimental import pallas as pl
from jax.experimental.pallas import tpu as pltpu
from jax.sharding import PartitionSpec as P

PERIODS = 44
DAMPING = 0.05
ROWS = 48
STEP = 32
PTS = 128
EARLY = 3
RESIDUES = (0, 2, 1, 3)
ROW_LANE = 64
RUP_LANE = 96
F32 = jnp.float32
BF16 = jnp.bfloat16


def nn(a, b):
    return lax.dot_general(a, b, (((1,), (0,)), ((), ())), preferred_element_type=F32)


def nt(a, b):
    return lax.dot_general(a, b, (((1,), (1,)), ((), ())), preferred_element_type=F32)


def iota(shape, dim):
    return lax.broadcasted_iota(jnp.int32, shape, dim)


def hilo(x):
    hi = x.astype(BF16)
    return hi, (x - hi.astype(F32)).astype(BF16)


def angle(product, n_time):
    return (2.0 * math.pi / n_time) * (product % n_time)


def cos_sin(*angles):
    return np.concatenate([f(x) for x in angles for f in (np.cos, np.sin)]).astype(np.float32)


def forward_base(n_time):
    index = np.arange(n_time // 8)
    freq = np.concatenate([4 * index + residue for residue in RESIDUES])
    coarse = angle(np.arange(n_time // 4 // STEP)[:, None] * STEP * freq[None, :], n_time)
    fine = angle(np.arange(STEP)[:, None] * freq[None, :], n_time)
    return cos_sin(coarse, fine)


def inverse_bases(n_time):
    time = np.arange(n_time // 4)
    coarse = angle(np.arange(n_time // 8 // STEP)[:, None] * 4 * STEP * time[None, :], n_time)
    fine = [
        angle((np.arange(STEP)[:, None] * 4 + residue) * time[None, :], n_time)
        for residue in RESIDUES
    ]
    return [cos_sin(coarse, *fine[:2]), cos_sin(coarse, *fine[2:])]


def ordered(stages, apart):
    place = jnp.zeros_like(apart["worker"])
    for axis, radix, shift, _ in stages:
        place = place * radix + ((apart[axis] >> shift) & (radix - 1))
    return place


def pack_kernel(*refs):
    sources = (*refs[:5], refs[5].at[:EARLY])
    out_ref, kept_ref, rows_ref, scr, own_ref, pts_ref, mom_ref, slip_ref, sems = refs[6:]
    copies = [
        pltpu.make_async_copy(src, dst, sems.at[i])
        for i, (src, dst) in enumerate(zip(sources, (own_ref, pts_ref, mom_ref, slip_ref, kept_ref, rows_ref)))
    ]
    for copy in copies:
        copy.start()
    devices, capacity, _ = out_ref.shape
    slots = devices * capacity
    rup_w, sub = pts_ref.shape
    asked = rup_w * sub
    n_slip = slip_ref.shape[2]
    earlier = (iota((asked, asked), 0) < iota((asked, asked), 1)).astype(F32).astype(BF16)
    spread = iota((128, 6), 0)
    comp = iota((128, 6), 1)
    spread_hi = (spread == comp).astype(F32).astype(BF16)
    spread_lo = (spread == comp + 6).astype(F32).astype(BF16)
    for copy in copies[:4]:
        copy.wait()
    own = own_ref[...]
    blocks = own.shape[0]
    both = jnp.concatenate([own // PTS, own % PTS], axis=0).astype(F32).astype(BF16)
    p = jnp.concatenate([pts_ref[r : r + 1, :] for r in range(rup_w)], axis=1)
    in_lane = (iota((128, asked), 0) == p % 128).astype(F32).astype(BF16)
    found = nn(both, in_lane)
    in_block = (iota((blocks, asked), 0) == p // 128).astype(F32)
    dev = jnp.sum(found[:blocks] * in_block, axis=0, keepdims=True)
    loc = jnp.sum(found[blocks:] * in_block, axis=0, keepdims=True)
    onehot = (iota((devices, asked), 0).astype(F32) == dev).astype(F32)
    before = nn(onehot.astype(BF16), earlier)
    rank = jnp.sum(before * onehot, axis=0, keepdims=True)
    target = dev * capacity + rank
    pick = (iota((slots, asked), 0).astype(F32) == target).astype(F32)
    pick16 = pick.astype(BF16)
    mom = jnp.concatenate(
        [
            jnp.concatenate([mom_ref[m, r : r + 1, :] for r in range(rup_w)], axis=1)
            for m in range(6)
        ],
        axis=0,
    )
    hi, lo = hilo(mom)
    rup = (iota((1, asked), 1) // sub).astype(F32)
    lane = iota((128, asked), 0)
    expanded = nn(spread_hi, hi) + nn(spread_lo, lo)
    expanded = jnp.where(lane == ROW_LANE, loc, jnp.where(lane == RUP_LANE, rup, expanded))
    scr[:, n_slip:] = nt(pick16, expanded.astype(BF16))
    slip = slip_ref[...].astype(F32).reshape(asked, n_slip).astype(BF16)
    scr[:, :n_slip] = nn(pick16, slip)
    for d in range(devices):
        out_ref[d] = scr[d * capacity : (d + 1) * capacity, :].astype(BF16)
    for copy in copies[4:]:
        copy.wait()


def forward_table(base_ref, tab_ref, block):
    count = tab_ref.shape[0] // STEP
    wide = tab_ref.shape[1] // 8
    sl = slice(block * wide, (block + 1) * wide)
    cols = slice(2 * block * wide, (2 * block + 1) * wide)
    cols_im = slice((2 * block + 1) * wide, (2 * block + 2) * wide)
    cb = base_ref[2 * count : 2 * count + STEP, sl]
    sb = base_ref[2 * count + STEP :, sl]

    def table(a, carry):
        ca = base_ref[pl.ds(a, 1), sl]
        sa = base_ref[pl.ds(count + a, 1), sl]
        at = pl.ds(pl.multiple_of(a * STEP, STEP), STEP)
        tab_ref[at, cols] = (ca * cb - sa * sb).astype(BF16)
        tab_ref[at, cols_im] = (-(sa * cb + ca * sb)).astype(BF16)
        return carry

    lax.fori_loop(0, count, table, 0, unroll=4)


def owner_kernel(stages, rec_ref, sgt_ref, base_ref, rows_ref, *refs):
    first = stages[0][1]
    out_refs = refs[:first]
    rec_s, x_s, p_s, slip_s, sgt_s, tab_s, sems = refs[first:]
    devices, capacity, width = rec_ref.shape
    slots = devices * capacity
    n_time = sgt_ref.shape[2]
    half = n_time // 2
    wide = n_time // 4
    block_wide = n_time // 8
    n_slip = width - 128
    copies = []
    for c in range(3):
        at = slice(6 * c if c else EARLY, 6 * c + 6)
        copies.append(pltpu.make_async_copy(sgt_ref.at[at], sgt_s.at[at], sems.at[c]))
        copies[c].start()
    for d in range(devices):
        rec_s[d * capacity : (d + 1) * capacity, :] = rec_ref[d].astype(F32)
    tail = rec_s[:, n_slip:]
    row = tail[:, ROW_LANE : ROW_LANE + 1]
    here = iota((slots, PTS), 1).astype(F32) == row
    left = jnp.concatenate(
        [
            jnp.concatenate(
                [jnp.where(here, tail[:, 6 * p + m : 6 * p + m + 1], 0.0).astype(BF16) for m in range(6)],
                axis=1,
            )
            for p in range(2)
        ],
        axis=0,
    )
    for block in range(4):
        forward_table(base_ref, tab_s, block)
    slip = rec_s[:, :n_slip].astype(BF16)
    for block in range(4):
        cols = slice(2 * block * block_wide, 2 * (block + 1) * block_wide)
        slip_s[:, cols] = nn(slip, tab_s[:, cols])
    ruptures = math.prod(radix for _, radix, _, _ in stages)
    shape = (ruptures, slots)
    rup = nt((iota((8, 128), 1) == RUP_LANE).astype(F32).astype(BF16), tail.astype(BF16))[:1].astype(jnp.int32)
    worker = (iota((1, slots), 1) // capacity) % lax.axis_size("worker")
    apart = {"worker": worker ^ lax.axis_index("worker"), "server": rup ^ lax.axis_index("server")}
    where_to = ordered(stages, apart)
    seg = (iota(shape, 0) == where_to).astype(F32).astype(BF16)
    seg = jnp.concatenate([seg, seg], axis=1)
    part = ruptures // first
    for c in range(3):
        copies[c].wait()
        x = []
        for k in range(4):
            cols = slice(k * wide, (k + 1) * wide)
            rows = sgt_s[6 * c if c else EARLY : 6 * c + 6, :, cols].reshape(-1, wide)
            if c == 0:
                rows = jnp.concatenate([rows_ref[:, :, cols].reshape(-1, wide), rows], axis=0)
            out = nn(left, rows)
            x.append(out[:slots] + out[slots:])
        plus = (x[0] + x[2], x[1] + x[3])
        x_s[c, :slots, :] = (plus[0] + plus[1]).astype(BF16)
        x_s[c, slots : 2 * slots, :] = (plus[0] - plus[1]).astype(BF16)
        x_s[c, 2 * slots : 3 * slots, :] = (x[0] - x[2]).astype(BF16)
        x_s[c, 3 * slots :, :] = (x[1] - x[3]).astype(BF16)
        for block in range(4):
            first_row, last_row = ((0, 1), (1, 2), (2, 4), (2, 4))[block]
            middle = (2 * block + 1) * block_wide
            cols = slice(middle - block_wide, middle)
            cols_im = slice(middle, middle + block_wide)
            product = nn(
                x_s[c, first_row * slots : last_row * slots, :],
                tab_s[:, middle - block_wide : middle + block_wide],
            )
            t_re = product[:slots, :block_wide]
            t_im = product[:slots, block_wide:]
            if block == 2:
                t_re, t_im = t_re + product[slots:, block_wide:], t_im - product[slots:, :block_wide]
            elif block == 3:
                t_re, t_im = t_re - product[slots:, block_wide:], t_im + product[slots:, :block_wide]
            slip_re = slip_s[:, cols]
            slip_im = slip_s[:, cols_im]
            hi, lo = hilo(slip_re * t_re - slip_im * t_im)
            p_s[:slots, cols] = hi
            p_s[slots:, cols] = lo
            hi, lo = hilo(slip_re * t_im + slip_im * t_re)
            p_s[:slots, cols_im] = hi
            p_s[slots:, cols_im] = lo
        total = nn(seg, p_s[...])
        for block in range(4):
            for k in range(first):
                ref = out_refs[k]
                for p in range(2):
                    at = slice(p * half + block * block_wide, p * half + (block + 1) * block_wide)
                    ref[c, :, at] = total[
                        k * part : (k + 1) * part, (2 * block + p) * block_wide : (2 * block + p + 1) * block_wide
                    ].astype(ref.dtype)


def sum_kernel(radix, *refs):
    own_ref = refs[0]
    out_refs = refs[-radix:]
    part = out_refs[0].shape[1]
    for c in range(3):
        total = own_ref[c]
        for ref in refs[1:-radix]:
            total = total + ref[c].astype(F32)
        for k in range(radix):
            out_refs[k][c] = total[k * part : (k + 1) * part].astype(out_refs[k].dtype)


def inverse_table_kernel(base_ref, tab_ref):
    block_wide = tab_ref.shape[0] // 4
    count = block_wide // STEP
    wide = 256
    for p in range(2):
        fine = 2 * count + 2 * p * STEP
        for lc in range(tab_ref.shape[1] // wide):
            sl = slice(lc * wide, (lc + 1) * wide)
            cf = base_ref[fine : fine + STEP, sl]
            sf = base_ref[fine + STEP : fine + 2 * STEP, sl]

            def table(a, carry):
                ca = base_ref[pl.ds(a, 1), sl]
                sa = base_ref[pl.ds(count + a, 1), sl]
                for base, value in ((0, ca * cf - sa * sf), (block_wide, -(sa * cf + ca * sf))):
                    at = pl.ds(pl.multiple_of(2 * p * block_wide + base + a * STEP, STEP), STEP)
                    tab_ref[at, sl] = value.astype(BF16)
                return carry

            lax.fori_loop(0, count, table, 0)


def gain_kernel(gr_ref, gi_ref):
    half = gr_ref.shape[1]
    block_wide = half // 4
    n_time = 2 * half
    shape = gr_ref.shape
    low = math.log(4.0 / n_time)
    high = math.log(0.25)
    period = iota(shape, 0)
    slot = iota(shape, 1)
    block = slot // block_wide
    freq = 4 * (slot % block_wide) + jnp.where(block < 2, 2 * block, 2 * block - 3)
    omega_freq = freq.astype(F32) * (2.0 * math.pi / n_time)
    omega_osc = 2.0 * math.pi * jnp.exp(low + (high - low) * period.astype(F32) / (PERIODS - 1))
    den_real = omega_osc * omega_osc - omega_freq * omega_freq
    den_imag = 2.0 * DAMPING * omega_osc * omega_freq
    weight = jnp.where(freq == 0, 1.0, 2.0) / n_time
    gain = weight * (omega_osc * omega_osc / (den_real * den_real + den_imag * den_imag))
    gr_ref[...] = jnp.where(period < PERIODS, -gain * den_real, weight)
    gi_ref[...] = jnp.where(period < PERIODS, -gain * den_imag, 0.0)


def final_kernel(count, *refs):
    spec_refs = refs[:count]
    *tables, gr_ref, gi_ref, seis_ref, peak_ref = refs[count:]
    half = gr_ref.shape[1]
    block_wide = half // 4
    wide = half // 2
    spec = []
    for c in range(3):
        total = spec_refs[0][c]
        for ref in spec_refs[1:]:
            total = total + ref[c].astype(F32)
        spec.append(total)
    gr = gr_ref[...]
    gi = gi_ref[...]

    def accel(block):
        cols = slice(block * block_wide, (block + 1) * block_wide)
        cols_im = slice(half + block * block_wide, half + (block + 1) * block_wide)
        g_re = gr[:, cols]
        g_im = gi[:, cols]
        re = jnp.concatenate([s[:, cols] * g_re + s[:, cols_im] * g_im for s in spec], axis=0)
        im = jnp.concatenate([s[:, cols_im] * g_re - s[:, cols] * g_im for s in spec], axis=0)
        return re, im

    def product(left, table):
        count = left.shape[0]
        both = nn(jnp.concatenate(hilo(left), axis=0), table)
        return both[:count] + both[count:]

    even_ref, odd_ref = tables
    pair = [
        product(
            jnp.concatenate(accel(block), axis=1),
            even_ref[block * wide : (block + 1) * wide, :],
        )
        for block in range(2)
    ]
    re_c, im_c = accel(2)
    re_d, im_d = accel(3)
    straight = jnp.concatenate([re_c, im_c, re_d, im_d], axis=1)
    turned = jnp.concatenate([-im_c, re_c, im_d, -re_d], axis=1)
    odd = product(jnp.concatenate([straight, turned], axis=0), odd_ref[...])
    evens = (pair[0] + pair[1], pair[0] - pair[1])
    odds = (odd[: 3 * ROWS], odd[3 * ROWS :])
    peak = jnp.max(
        jnp.maximum(jnp.abs(evens[0]) + jnp.abs(odds[0]), jnp.abs(evens[1]) + jnp.abs(odds[1])),
        axis=1,
        keepdims=True,
    )
    for c in range(3):
        row = c * ROWS + PERIODS
        for k in range(2):
            e = evens[k][row : row + 1]
            o = odds[k][row : row + 1]
            seis_ref[c, :, k * wide : (k + 1) * wide] = e + o
            seis_ref[c, :, half + k * wide : half + (k + 1) * wide] = e - o
        column = jnp.broadcast_to(peak[c * ROWS : (c + 1) * ROWS], (ROWS, 128))
        column = jnp.concatenate([column, jnp.zeros((128 - ROWS, 128), F32)], axis=0)
        peak_ref[c] = column.T[:1, :PERIODS]


def vmem():
    return pl.BlockSpec(memory_space=pltpu.VMEM)


def hbm():
    return pl.BlockSpec(memory_space=pltpu.HBM)


def in_hbm(x):
    return pltpu.with_memory_space_constraint(x, pltpu.HBM)


def params(mib):
    return pltpu.CompilerParams(vmem_limit_bytes=mib << 20)


def exchange_plan(n_worker, n_server):
    stages = []
    for axis, size in (("worker", n_worker), ("server", n_server)):
        bits = size.bit_length() - 1
        assert size == 1 << bits
        shift = 0
        while shift < bits:
            step = 1 if (bits - shift) % 2 else 2
            stages.append((axis, 1 << step, shift, size))
            shift += step
    return stages


def send(parts, stage):
    axis, radix, shift, size = stage
    return [
        lax.ppermute(parts[k], axis, [(i, i ^ (k << shift)) for i in range(size)])
        for k in range(radix - 1, 0, -1)
    ]


def beside(kernel, base, own):
    base, own = lax.optimization_barrier((jnp.asarray(base), own))
    own, *made = lax.optimization_barrier((own, *kernel(base)))
    return own, made


def sent_type(stages, i):
    return F32 if i == 0 or i == len(stages) - 1 else BF16


def shards(n_server, n_worker, sgt, ownership, sub_points, moments, slip):
    devices = n_server * n_worker
    n_time = sgt.shape[2]
    half = n_time // 2
    rup_w = sub_points.shape[1]
    sub_dev = sub_points.shape[2]
    n_slip = slip.shape[3]
    capacity = 4 * sub_dev // (3 * n_worker)
    slots = devices * capacity
    width = n_slip + 128
    stages = exchange_plan(n_worker, n_server)
    assert rup_w == n_server and sgt.shape[0] == PTS and slots % 16 == 0 and 4 * n_slip == n_time

    base = jnp.asarray(forward_base(n_time))
    sgt = in_hbm(jnp.transpose(sgt, (1, 0, 2)))
    record, base, rows = pl.pallas_call(
        pack_kernel,
        out_shape=[
            jax.ShapeDtypeStruct((devices, capacity, width), BF16),
            jax.ShapeDtypeStruct(base.shape, F32),
            jax.ShapeDtypeStruct((EARLY, PTS, n_time), BF16),
        ],
        in_specs=[hbm()] * 6,
        out_specs=[vmem()] * 3,
        scratch_shapes=[
            pltpu.VMEM((slots, width), F32),
            pltpu.VMEM((ownership.shape[0] // 128, 128), jnp.int32),
            pltpu.VMEM((rup_w, sub_dev), jnp.int32),
            pltpu.VMEM((6, rup_w, sub_dev), F32),
            pltpu.VMEM((rup_w, sub_dev, n_slip), BF16),
            pltpu.SemaphoreType.DMA((6,)),
        ],
        compiler_params=params(16),
        name="pack",
    )(
        *[
            in_hbm(x)
            for x in (
                ownership.reshape(-1, 128),
                sub_points[0],
                jnp.transpose(moments[0], (1, 0, 2)),
                slip[0],
                base,
                sgt,
            )
        ]
    )
    record = lax.all_to_all(record, ("server", "worker"), split_axis=0, concat_axis=0, tiled=True)

    inverse = pl.pallas_call(
        inverse_table_kernel,
        out_shape=[jax.ShapeDtypeStruct((half, half // 2), BF16)],
        in_specs=[vmem()],
        out_specs=[vmem()],
        compiler_params=params(8),
        cost_estimate=pl.CostEstimate(flops=10**9, bytes_accessed=10**7, transcendentals=0),
        name="inverse_table",
    )
    gain = pl.pallas_call(
        gain_kernel,
        out_shape=[jax.ShapeDtypeStruct((ROWS, half), F32)] * 2,
        out_specs=[vmem()] * 2,
        compiler_params=params(2),
        name="gain",
    )()
    tables = []
    bases = inverse_bases(n_time)

    def part_shapes(i):
        count = math.prod(radix for _, radix, _, _ in stages[i + 1 :])
        return [
            jax.ShapeDtypeStruct((3, count, n_time), sent_type(stages, i) if k else F32)
            for k in range(stages[i][1])
        ]

    parts = pl.pallas_call(
        functools.partial(owner_kernel, stages),
        out_shape=part_shapes(0),
        in_specs=[vmem(), hbm(), vmem(), vmem()],
        out_specs=[vmem()] * stages[0][1],
        scratch_shapes=[
            pltpu.VMEM((slots, width), F32),
            pltpu.VMEM((3, 4 * slots, n_slip), BF16),
            pltpu.VMEM((2 * slots, n_time), BF16),
            pltpu.VMEM((slots, n_time), F32),
            pltpu.VMEM((18, PTS, n_time), BF16),
            pltpu.VMEM((half // 2, n_time), BF16),
            pltpu.SemaphoreType.DMA((4,)),
        ],
        compiler_params=params(36),
        cost_estimate=pl.CostEstimate(flops=10**10, bytes_accessed=2 * 10**7, transcendentals=0),
        name="owner",
    )(record, sgt, base, rows)
    arrived = send(parts, stages[0])
    for i in range(1, len(stages)):
        radix = stages[i][1]
        parts = pl.pallas_call(
            functools.partial(sum_kernel, radix),
            out_shape=part_shapes(i),
            in_specs=[vmem()] * (1 + len(arrived)),
            out_specs=[vmem()] * radix,
            compiler_params=params(4),
            name=f"sum_{i}",
        )(parts[0], *arrived)
        arrived = send(parts, stages[i])
        if i >= len(stages) - 2:
            own, pair = beside(inverse, bases[len(tables)], parts[0])
            parts = [own]
            tables += pair
    count = 1 + len(arrived)
    seis, peaks = pl.pallas_call(
        functools.partial(final_kernel, count),
        out_shape=[
            jax.ShapeDtypeStruct((3, 1, n_time), F32),
            jax.ShapeDtypeStruct((3, 1, PERIODS), F32),
        ],
        in_specs=[vmem()] * (count + 4),
        out_specs=[vmem()] * 2,
        compiler_params=params(20),
        name="finish",
    )(parts[0], *arrived, *tables, *gain)
    return (
        jnp.transpose(seis, (1, 0, 2)).reshape(1, 1, 3, n_time),
        jnp.transpose(peaks, (1, 0, 2)).reshape(1, 1, 3, PERIODS),
    )


def solution(mesh):
    placed = (
        P(("server", "worker"), None, None),
        P(),
        P("worker", None, "server"),
        P("worker", None, None, "server"),
        P("worker", None, "server", None),
    )
    return jax.shard_map(
        functools.partial(shards, mesh.shape["server"], mesh.shape["worker"]),
        mesh=mesh,
        in_specs=placed,
        out_specs=(P("worker", "server", None, None), P("worker", "server", None, None)),
        check_vma=False,
    )
```

```python
import functools
import math

import jax
import jax.numpy as jnp
import numpy as np
from jax import lax
from jax.experimental import pallas as pl
from jax.experimental.pallas import tpu as pltpu
from jax.sharding import PartitionSpec as P

PERIODS = 44
DAMPING = 0.05
ROWS = 48
STEP = 32
PTS = 128
EARLY = 3
RESIDUES = (0, 2, 1, 3)
ROW_LANE = 64
RUP_LANE = 96
F32 = jnp.float32
BF16 = jnp.bfloat16


def nn(a, b):
    return lax.dot_general(a, b, (((1,), (0,)), ((), ())), preferred_element_type=F32)


def nt(a, b):
    return lax.dot_general(a, b, (((1,), (1,)), ((), ())), preferred_element_type=F32)


def iota(shape, dim):
    return lax.broadcasted_iota(jnp.int32, shape, dim)


def hilo(x):
    hi = x.astype(BF16)
    return hi, (x - hi.astype(F32)).astype(BF16)


def angle(product, n_time):
    return (2.0 * math.pi / n_time) * (product % n_time)


def cos_sin(*angles):
    return np.concatenate([f(x) for x in angles for f in (np.cos, np.sin)]).astype(np.float32)


def forward_base(n_time):
    index = np.arange(n_time // 8)
    freq = np.concatenate([4 * index + residue for residue in RESIDUES])
    coarse = angle(np.arange(n_time // 4 // STEP)[:, None] * STEP * freq[None, :], n_time)
    fine = angle(np.arange(STEP)[:, None] * freq[None, :], n_time)
    return cos_sin(coarse, fine)


def inverse_bases(n_time):
    time = np.arange(n_time // 4)
    coarse = angle(np.arange(n_time // 8 // STEP)[:, None] * 4 * STEP * time[None, :], n_time)
    fine = [
        angle((np.arange(STEP)[:, None] * 4 + residue) * time[None, :], n_time)
        for residue in RESIDUES
    ]
    return [cos_sin(coarse, *fine[:2]), cos_sin(coarse, *fine[2:])]


def ordered(stages, apart):
    place = jnp.zeros_like(apart["worker"])
    for axis, radix, shift, _ in stages:
        place = place * radix + ((apart[axis] >> shift) & (radix - 1))
    return place


def pack_kernel(*refs):
    sources = (*refs[:5], refs[5].at[:EARLY])
    out_ref, kept_ref, rows_ref, scr, own_ref, pts_ref, mom_ref, slip_ref, sems = refs[6:]
    copies = [
        pltpu.make_async_copy(src, dst, sems.at[i])
        for i, (src, dst) in enumerate(zip(sources, (own_ref, pts_ref, mom_ref, slip_ref, kept_ref, rows_ref)))
    ]
    for copy in copies:
        copy.start()
    devices, capacity, _ = out_ref.shape
    slots = devices * capacity
    rup_w, sub = pts_ref.shape
    asked = rup_w * sub
    n_slip = slip_ref.shape[2]
    earlier = (iota((asked, asked), 0) < iota((asked, asked), 1)).astype(F32).astype(BF16)
    spread = iota((128, 6), 0)
    comp = iota((128, 6), 1)
    spread_hi = (spread == comp).astype(F32).astype(BF16)
    spread_lo = (spread == comp + 6).astype(F32).astype(BF16)
    for copy in copies[:4]:
        copy.wait()
    own = own_ref[...]
    blocks = own.shape[0]
    both = jnp.concatenate([own // PTS, own % PTS], axis=0).astype(F32).astype(BF16)
    p = jnp.concatenate([pts_ref[r : r + 1, :] for r in range(rup_w)], axis=1)
    in_lane = (iota((128, asked), 0) == p % 128).astype(F32).astype(BF16)
    found = nn(both, in_lane)
    in_block = (iota((blocks, asked), 0) == p // 128).astype(F32)
    dev = jnp.sum(found[:blocks] * in_block, axis=0, keepdims=True)
    loc = jnp.sum(found[blocks:] * in_block, axis=0, keepdims=True)
    onehot = (iota((devices, asked), 0).astype(F32) == dev).astype(F32)
    before = nn(onehot.astype(BF16), earlier)
    rank = jnp.sum(before * onehot, axis=0, keepdims=True)
    target = dev * capacity + rank
    pick = (iota((slots, asked), 0).astype(F32) == target).astype(F32)
    pick16 = pick.astype(BF16)
    mom = jnp.concatenate(
        [
            jnp.concatenate([mom_ref[m, r : r + 1, :] for r in range(rup_w)], axis=1)
            for m in range(6)
        ],
        axis=0,
    )
    hi, lo = hilo(mom)
    rup = (iota((1, asked), 1) // sub).astype(F32)
    lane = iota((128, asked), 0)
    expanded = nn(spread_hi, hi) + nn(spread_lo, lo)
    expanded = jnp.where(lane == ROW_LANE, loc, jnp.where(lane == RUP_LANE, rup, expanded))
    scr[:, n_slip:] = nt(pick16, expanded.astype(BF16))
    slip = slip_ref[...].astype(F32).reshape(asked, n_slip).astype(BF16)
    scr[:, :n_slip] = nn(pick16, slip)
    for d in range(devices):
        out_ref[d] = scr[d * capacity : (d + 1) * capacity, :].astype(BF16)
    for copy in copies[4:]:
        copy.wait()


def forward_table(base_ref, tab_ref, block):
    count = tab_ref.shape[0] // STEP
    wide = tab_ref.shape[1] // 8
    sl = slice(block * wide, (block + 1) * wide)
    cols = slice(2 * block * wide, (2 * block + 1) * wide)
    cols_im = slice((2 * block + 1) * wide, (2 * block + 2) * wide)
    cb = base_ref[2 * count : 2 * count + STEP, sl]
    sb = base_ref[2 * count + STEP :, sl]

    def table(a, carry):
        ca = base_ref[pl.ds(a, 1), sl]
        sa = base_ref[pl.ds(count + a, 1), sl]
        at = pl.ds(pl.multiple_of(a * STEP, STEP), STEP)
        tab_ref[at, cols] = (ca * cb - sa * sb).astype(BF16)
        tab_ref[at, cols_im] = (-(sa * cb + ca * sb)).astype(BF16)
        return carry

    lax.fori_loop(0, count, table, 0, unroll=4)


def owner_kernel(stages, rec_ref, sgt_ref, base_ref, rows_ref, *refs):
    first = stages[0][1]
    out_refs = refs[:first]
    rec_s, x_s, p_s, slip_s, sgt_s, tab_s, sems = refs[first:]
    devices, capacity, width = rec_ref.shape
    slots = devices * capacity
    n_time = sgt_ref.shape[2]
    half = n_time // 2
    wide = n_time // 4
    block_wide = n_time // 8
    n_slip = width - 128
    copies = []
    for c in range(3):
        at = slice(6 * c if c else EARLY, 6 * c + 6)
        copies.append(pltpu.make_async_copy(sgt_ref.at[at], sgt_s.at[at], sems.at[c]))
        copies[c].start()
    for d in range(devices):
        rec_s[d * capacity : (d + 1) * capacity, :] = rec_ref[d].astype(F32)
    tail = rec_s[:, n_slip:]
    row = tail[:, ROW_LANE : ROW_LANE + 1]
    here = iota((slots, PTS), 1).astype(F32) == row
    left = jnp.concatenate(
        [
            jnp.concatenate(
                [jnp.where(here, tail[:, 6 * p + m : 6 * p + m + 1], 0.0).astype(BF16) for m in range(6)],
                axis=1,
            )
            for p in range(2)
        ],
        axis=0,
    )
    for block in range(4):
        forward_table(base_ref, tab_s, block)
    slip = rec_s[:, :n_slip].astype(BF16)
    for block in range(4):
        cols = slice(2 * block * block_wide, 2 * (block + 1) * block_wide)
        slip_s[:, cols] = nn(slip, tab_s[:, cols])
    ruptures = math.prod(radix for _, radix, _, _ in stages)
    shape = (ruptures, slots)
    rup = nt((iota((8, 128), 1) == RUP_LANE).astype(F32).astype(BF16), tail.astype(BF16))[:1].astype(jnp.int32)
    worker = (iota((1, slots), 1) // capacity) % lax.axis_size("worker")
    apart = {"worker": worker ^ lax.axis_index("worker"), "server": rup ^ lax.axis_index("server")}
    where_to = ordered(stages, apart)
    seg = (iota(shape, 0) == where_to).astype(F32).astype(BF16)
    seg = jnp.concatenate([seg, seg], axis=1)
    part = ruptures // first
    for c in range(3):
        copies[c].wait()
        x = []
        for k in range(4):
            cols = slice(k * wide, (k + 1) * wide)
            rows = sgt_s[6 * c if c else EARLY : 6 * c + 6, :, cols].reshape(-1, wide)
            if c == 0:
                rows = jnp.concatenate([rows_ref[:, :, cols].reshape(-1, wide), rows], axis=0)
            out = nn(left, rows)
            x.append(out[:slots] + out[slots:])
        plus = (x[0] + x[2], x[1] + x[3])
        x_s[c, :slots, :] = (plus[0] + plus[1]).astype(BF16)
        x_s[c, slots : 2 * slots, :] = (plus[0] - plus[1]).astype(BF16)
        x_s[c, 2 * slots : 3 * slots, :] = (x[0] - x[2]).astype(BF16)
        x_s[c, 3 * slots :, :] = (x[1] - x[3]).astype(BF16)
        for block in range(4):
            first_row, last_row = ((0, 1), (1, 2), (2, 4), (2, 4))[block]
            middle = (2 * block + 1) * block_wide
            cols = slice(middle - block_wide, middle)
            cols_im = slice(middle, middle + block_wide)
            product = nn(
                x_s[c, first_row * slots : last_row * slots, :],
                tab_s[:, middle - block_wide : middle + block_wide],
            )
            t_re = product[:slots, :block_wide]
            t_im = product[:slots, block_wide:]
            if block == 2:
                t_re, t_im = t_re + product[slots:, block_wide:], t_im - product[slots:, :block_wide]
            elif block == 3:
                t_re, t_im = t_re - product[slots:, block_wide:], t_im + product[slots:, :block_wide]
            slip_re = slip_s[:, cols]
            slip_im = slip_s[:, cols_im]
            hi, lo = hilo(slip_re * t_re - slip_im * t_im)
            p_s[:slots, cols] = hi
            p_s[slots:, cols] = lo
            hi, lo = hilo(slip_re * t_im + slip_im * t_re)
            p_s[:slots, cols_im] = hi
            p_s[slots:, cols_im] = lo
        total = nn(seg, p_s[...])
        for block in range(4):
            for k in range(first):
                ref = out_refs[k]
                for p in range(2):
                    at = slice(p * half + block * block_wide, p * half + (block + 1) * block_wide)
                    ref[c, :, at] = total[
                        k * part : (k + 1) * part, (2 * block + p) * block_wide : (2 * block + p + 1) * block_wide
                    ].astype(ref.dtype)


def sum_kernel(radix, *refs):
    own_ref = refs[0]
    out_refs = refs[-radix:]
    part = out_refs[0].shape[1]
    for c in range(3):
        total = own_ref[c]
        for ref in refs[1:-radix]:
            total = total + ref[c].astype(F32)
        for k in range(radix):
            out_refs[k][c] = total[k * part : (k + 1) * part].astype(out_refs[k].dtype)


def inverse_table_kernel(base_ref, tab_ref):
    block_wide = tab_ref.shape[0] // 4
    count = block_wide // STEP
    wide = 256
    for p in range(2):
        fine = 2 * count + 2 * p * STEP
        for lc in range(tab_ref.shape[1] // wide):
            sl = slice(lc * wide, (lc + 1) * wide)
            cf = base_ref[fine : fine + STEP, sl]
            sf = base_ref[fine + STEP : fine + 2 * STEP, sl]

            def table(a, carry):
                ca = base_ref[pl.ds(a, 1), sl]
                sa = base_ref[pl.ds(count + a, 1), sl]
                for base, value in ((0, ca * cf - sa * sf), (block_wide, -(sa * cf + ca * sf))):
                    at = pl.ds(pl.multiple_of(2 * p * block_wide + base + a * STEP, STEP), STEP)
                    tab_ref[at, sl] = value.astype(BF16)
                return carry

            lax.fori_loop(0, count, table, 0)


def gain_kernel(gr_ref, gi_ref):
    half = gr_ref.shape[1]
    block_wide = half // 4
    n_time = 2 * half
    shape = gr_ref.shape
    low = math.log(4.0 / n_time)
    high = math.log(0.25)
    period = iota(shape, 0)
    slot = iota(shape, 1)
    block = slot // block_wide
    freq = 4 * (slot % block_wide) + jnp.where(block < 2, 2 * block, 2 * block - 3)
    omega_freq = freq.astype(F32) * (2.0 * math.pi / n_time)
    omega_osc = 2.0 * math.pi * jnp.exp(low + (high - low) * period.astype(F32) / (PERIODS - 1))
    den_real = omega_osc * omega_osc - omega_freq * omega_freq
    den_imag = 2.0 * DAMPING * omega_osc * omega_freq
    weight = jnp.where(freq == 0, 1.0, 2.0) / n_time
    gain = weight * (omega_osc * omega_osc / (den_real * den_real + den_imag * den_imag))
    gr_ref[...] = jnp.where(period < PERIODS, -gain * den_real, weight)
    gi_ref[...] = jnp.where(period < PERIODS, -gain * den_imag, 0.0)


def final_kernel(count, *refs):
    spec_refs = refs[:count]
    *tables, gr_ref, gi_ref, seis_ref, peak_ref = refs[count:]
    half = gr_ref.shape[1]
    block_wide = half // 4
    wide = half // 2
    spec = []
    for c in range(3):
        total = spec_refs[0][c]
        for ref in spec_refs[1:]:
            total = total + ref[c].astype(F32)
        spec.append(total)
    gr = gr_ref[...]
    gi = gi_ref[...]

    def accel(block):
        cols = slice(block * block_wide, (block + 1) * block_wide)
        cols_im = slice(half + block * block_wide, half + (block + 1) * block_wide)
        g_re = gr[:, cols]
        g_im = gi[:, cols]
        re = jnp.concatenate([s[:, cols] * g_re + s[:, cols_im] * g_im for s in spec], axis=0)
        im = jnp.concatenate([s[:, cols_im] * g_re - s[:, cols] * g_im for s in spec], axis=0)
        return re, im

    def product(left, table):
        count = left.shape[0]
        both = nn(jnp.concatenate(hilo(left), axis=0), table)
        return both[:count] + both[count:]

    even_ref, odd_ref = tables
    pair = [
        product(
            jnp.concatenate(accel(block), axis=1),
            even_ref[block * wide : (block + 1) * wide, :],
        )
        for block in range(2)
    ]
    re_c, im_c = accel(2)
    re_d, im_d = accel(3)
    straight = jnp.concatenate([re_c, im_c, re_d, im_d], axis=1)
    turned = jnp.concatenate([-im_c, re_c, im_d, -re_d], axis=1)
    odd = product(jnp.concatenate([straight, turned], axis=0), odd_ref[...])
    evens = (pair[0] + pair[1], pair[0] - pair[1])
    odds = (odd[: 3 * ROWS], odd[3 * ROWS :])
    peak = jnp.max(
        jnp.maximum(jnp.abs(evens[0]) + jnp.abs(odds[0]), jnp.abs(evens[1]) + jnp.abs(odds[1])),
        axis=1,
        keepdims=True,
    )
    for c in range(3):
        row = c * ROWS + PERIODS
        for k in range(2):
            e = evens[k][row : row + 1]
            o = odds[k][row : row + 1]
            seis_ref[c, :, k * wide : (k + 1) * wide] = e + o
            seis_ref[c, :, half + k * wide : half + (k + 1) * wide] = e - o
        column = jnp.broadcast_to(peak[c * ROWS : (c + 1) * ROWS], (ROWS, 128))
        column = jnp.concatenate([column, jnp.zeros((128 - ROWS, 128), F32)], axis=0)
        peak_ref[c] = column.T[:1, :PERIODS]


def vmem():
    return pl.BlockSpec(memory_space=pltpu.VMEM)


def hbm():
    return pl.BlockSpec(memory_space=pltpu.HBM)


def in_hbm(x):
    return pltpu.with_memory_space_constraint(x, pltpu.HBM)


def params(mib):
    return pltpu.CompilerParams(vmem_limit_bytes=mib << 20)


def exchange_plan(n_worker, n_server):
    stages = []
    for axis, size in (("worker", n_worker), ("server", n_server)):
        bits = size.bit_length() - 1
        assert size == 1 << bits
        shift = 0
        while shift < bits:
            step = 1 if (bits - shift) % 2 else 2
            stages.append((axis, 1 << step, shift, size))
            shift += step
    return stages


def send(parts, stage):
    axis, radix, shift, size = stage
    return [
        lax.ppermute(parts[k], axis, [(i, i ^ (k << shift)) for i in range(size)])
        for k in range(radix - 1, 0, -1)
    ]


def beside(kernel, base, own):
    base, own = lax.optimization_barrier((jnp.asarray(base), own))
    own, *made = lax.optimization_barrier((own, *kernel(base)))
    return own, made


def sent_type(stages, i):
    return F32 if i == len(stages) - 1 else BF16


def shards(n_server, n_worker, sgt, ownership, sub_points, moments, slip):
    devices = n_server * n_worker
    n_time = sgt.shape[2]
    half = n_time // 2
    rup_w = sub_points.shape[1]
    sub_dev = sub_points.shape[2]
    n_slip = slip.shape[3]
    capacity = 4 * sub_dev // (3 * n_worker)
    slots = devices * capacity
    width = n_slip + 128
    stages = exchange_plan(n_worker, n_server)
    assert rup_w == n_server and sgt.shape[0] == PTS and slots % 16 == 0 and 4 * n_slip == n_time

    base = jnp.asarray(forward_base(n_time))
    sgt = in_hbm(jnp.transpose(sgt, (1, 0, 2)))
    record, base, rows = pl.pallas_call(
        pack_kernel,
        out_shape=[
            jax.ShapeDtypeStruct((devices, capacity, width), BF16),
            jax.ShapeDtypeStruct(base.shape, F32),
            jax.ShapeDtypeStruct((EARLY, PTS, n_time), BF16),
        ],
        in_specs=[hbm()] * 6,
        out_specs=[vmem()] * 3,
        scratch_shapes=[
            pltpu.VMEM((slots, width), F32),
            pltpu.VMEM((ownership.shape[0] // 128, 128), jnp.int32),
            pltpu.VMEM((rup_w, sub_dev), jnp.int32),
            pltpu.VMEM((6, rup_w, sub_dev), F32),
            pltpu.VMEM((rup_w, sub_dev, n_slip), BF16),
            pltpu.SemaphoreType.DMA((6,)),
        ],
        compiler_params=params(16),
        name="pack",
    )(
        *[
            in_hbm(x)
            for x in (
                ownership.reshape(-1, 128),
                sub_points[0],
                jnp.transpose(moments[0], (1, 0, 2)),
                slip[0],
                base,
                sgt,
            )
        ]
    )
    record = lax.all_to_all(record, ("server", "worker"), split_axis=0, concat_axis=0, tiled=True)

    inverse = pl.pallas_call(
        inverse_table_kernel,
        out_shape=[jax.ShapeDtypeStruct((half, half // 2), BF16)],
        in_specs=[vmem()],
        out_specs=[vmem()],
        compiler_params=params(8),
        cost_estimate=pl.CostEstimate(flops=10**9, bytes_accessed=10**7, transcendentals=0),
        name="inverse_table",
    )
    gain = pl.pallas_call(
        gain_kernel,
        out_shape=[jax.ShapeDtypeStruct((ROWS, half), F32)] * 2,
        out_specs=[vmem()] * 2,
        compiler_params=params(2),
        name="gain",
    )()
    tables = []
    bases = inverse_bases(n_time)

    def part_shapes(i):
        count = math.prod(radix for _, radix, _, _ in stages[i + 1 :])
        return [
            jax.ShapeDtypeStruct((3, count, n_time), sent_type(stages, i) if k else F32)
            for k in range(stages[i][1])
        ]

    parts = pl.pallas_call(
        functools.partial(owner_kernel, stages),
        out_shape=part_shapes(0),
        in_specs=[vmem(), hbm(), vmem(), vmem()],
        out_specs=[vmem()] * stages[0][1],
        scratch_shapes=[
            pltpu.VMEM((slots, width), F32),
            pltpu.VMEM((3, 4 * slots, n_slip), BF16),
            pltpu.VMEM((2 * slots, n_time), BF16),
            pltpu.VMEM((slots, n_time), F32),
            pltpu.VMEM((18, PTS, n_time), BF16),
            pltpu.VMEM((half // 2, n_time), BF16),
            pltpu.SemaphoreType.DMA((4,)),
        ],
        compiler_params=params(36),
        cost_estimate=pl.CostEstimate(flops=10**10, bytes_accessed=2 * 10**7, transcendentals=0),
        name="owner",
    )(record, sgt, base, rows)
    arrived = send(parts, stages[0])
    for i in range(1, len(stages)):
        radix = stages[i][1]
        parts = pl.pallas_call(
            functools.partial(sum_kernel, radix),
            out_shape=part_shapes(i),
            in_specs=[vmem()] * (1 + len(arrived)),
            out_specs=[vmem()] * radix,
            compiler_params=params(4),
            name=f"sum_{i}",
        )(parts[0], *arrived)
        arrived = send(parts, stages[i])
        if i >= len(stages) - 2:
            own, pair = beside(inverse, bases[len(tables)], parts[0])
            parts = [own]
            tables += pair
    count = 1 + len(arrived)
    seis, peaks = pl.pallas_call(
        functools.partial(final_kernel, count),
        out_shape=[
            jax.ShapeDtypeStruct((3, 1, n_time), F32),
            jax.ShapeDtypeStruct((3, 1, PERIODS), F32),
        ],
        in_specs=[vmem()] * (count + 4),
        out_specs=[vmem()] * 2,
        compiler_params=params(20),
        name="finish",
    )(parts[0], *arrived, *tables, *gain)
    return (
        jnp.transpose(seis, (1, 0, 2)).reshape(1, 1, 3, n_time),
        jnp.transpose(peaks, (1, 0, 2)).reshape(1, 1, 3, PERIODS),
    )


def solution(mesh):
    placed = (
        P(("server", "worker"), None, None),
        P(),
        P("worker", None, "server"),
        P("worker", None, None, "server"),
        P("worker", None, "server", None),
    )
    return jax.shard_map(
        functools.partial(shards, mesh.shape["server"], mesh.shape["worker"]),
        mesh=mesh,
        in_specs=placed,
        out_specs=(P("worker", "server", None, None), P("worker", "server", None, None)),
        check_vma=False,
    )
```
